32 devices in a mesh: parts: 2 (over y), az: 4 (over z), date: 2 (over x), rg: 2 (over core).
Axes of the slice: x: 2, y: 2, z: 4, core: 2. Of those that a mesh axis runs over, the one named last changes fastest.
Arguments:
- image_stack: float32 [2, 4, 256, 512], P(None, ('parts', 'date'), 'az', 'rg'), parts along dimension 1, may hold values from -6 to 6
- tap_weights: float32 [8, 4, 256], P(None, ('parts', 'date'), 'az'), parts along dimension 1, may hold values from -0.25 to 0.75
- offsets: int32 [4, 256], P(('parts', 'date'), 'az'), parts along dimension 0, may hold values from -12 to 12, as said below
- matchings: int32 [3, 2], replicated, may hold values from 0 to 1, each once within a row
Outputs:
- filtered: float32 [3, 2, 4, 256, 512], P(None, None, ('parts', 'date'), 'az', 'rg'), parts along dimension 2
The draws below stay inside these ranges and needn't reach their ends.
There are 2 independent parts, one for each index of `parts`. The reference program is written for one: setup_inputs(seed, part) draws one part's arguments, and reference() takes and returns one part's arrays. A program takes and returns all parts, laid end to end along the dimension named above; an argument that names none is the same for every part. Nothing has to cross between parts.
Inputs may be any that keep to these rules, and one draw needn't show every extreme that they name: `offsets`: both ends of the range occur in every draw. `matchings`: each row names every date once.
All inputs are finite; a program needn't handle non-finite values.
Results may differ from the reference program's by a relative error of at most 0.0045.
Values may be sent and summed in bfloat16 or wider, within the bound.
A program may use at most 64 MiB of HBM per device.

```python
import math
import jax
import jax.numpy as jnp
from jax import lax

TAPS = 8
SHIFT_MAX = 12
MATCHES = 3
PATCH = 64
DATES = 2
LINES = 256
SAMPLES = 512


def draw_offsets(key, part):
    random_base = jax.random.randint(jax.random.fold_in(key, 11), (DATES * LINES,), -SHIFT_MAX, SHIFT_MAX + 1, dtype=jnp.int32)
    spot_first = jax.random.randint(jax.random.fold_in(key, 12), (), 0, DATES * LINES, dtype=jnp.int32)
    spot_step = jax.random.randint(jax.random.fold_in(key, 13), (), 1, DATES * LINES, dtype=jnp.int32)
    spot_second = (spot_first + spot_step) % (DATES * LINES)
    flat_values = random_base.at[spot_first].set(SHIFT_MAX)
    flat_values = flat_values.at[spot_second].set(-SHIFT_MAX)
    return flat_values.reshape(DATES, LINES)


def steps_of(stream_key, dims, pieces, low, largest):
    factor_of, own = 1.0, jax.random.fold_in(stream_key, 6)
    for axis_at, shards_of in pieces:
        draws = jnp.exp(jax.random.uniform(jax.random.fold_in(own, axis_at), (shards_of,), jnp.float32, low / len(pieces), largest / len(pieces)))
        factor_of = factor_of * jnp.repeat(draws, dims[axis_at] // shards_of).reshape([-1 if axis == axis_at else 1 for axis in range(len(dims))])
    return factor_of


def noise(stream_key, shape, spread, limit, pieces=(), held_as=jnp.bfloat16):
    level = steps_of(stream_key, shape, pieces, -0.22, 0.18) if pieces else 1.0
    values = jax.random.normal(stream_key, shape, jnp.float32) * spread * level
    return jnp.minimum(jnp.maximum(values, -limit), limit).astype(held_as)


def setup_inputs(seed: int = 0, part: int = 0) -> dict:
    streams_of = jax.random.split(jax.random.key(seed), 5)
    own_keys = jax.random.split(jax.random.fold_in(streams_of[4], part), 5)
    return {
        "image_stack": noise(own_keys[0], (2, DATES, LINES, SAMPLES), 1.0, 6.0, ((1, 2), (2, 4), (3, 2)), jnp.float32),
        "tap_weights": jnp.clip(-0.25 + 1.0 * jax.random.uniform(own_keys[1], (TAPS, DATES, LINES), jnp.float32) ** steps_of(own_keys[1], (TAPS, DATES, LINES), ((1, 2), (2, 4)), -0.2, 0.2), -0.25, 0.75),
        "offsets": draw_offsets(jax.random.fold_in(jax.random.fold_in(streams_of[4], part), 71), part),
        "matchings": jax.vmap(lambda own: jax.random.permutation(own, DATES))(jax.random.split(streams_of[3], MATCHES)).reshape((MATCHES, DATES)).astype(jnp.int32),
    }


def fourier_table(sine_sign, table_scale):
    freq_ids = jnp.arange(PATCH, dtype=jnp.int32)
    phase_ids = (freq_ids[:, None] * freq_ids[None, :]) % PATCH
    angles = phase_ids.astype(jnp.float32) * (2.0 * math.pi / PATCH)
    cosine = jnp.cos(angles) * table_scale
    sine_part = jnp.sin(angles) * (sine_sign * table_scale)
    upper_rows = jnp.concatenate([cosine, -sine_part], axis=1)
    bottom = jnp.concatenate([sine_part, cosine], axis=1)
    return jnp.concatenate([upper_rows, bottom], axis=0).astype(jnp.bfloat16)


def patch_window():
    return jnp.sin(math.pi * (jnp.arange(PATCH, dtype=jnp.float32) + 0.5) / PATCH) ** 2


def filter_rows(band_rows, forward_table, inverse_table, window):
    half_patch = PATCH // 2
    width = band_rows.shape[1]
    line_spectra = jnp.dot(forward_table.T, band_rows, preferred_element_type=jnp.float32).astype(jnp.bfloat16)
    blocks = line_spectra.reshape(2, PATCH, width // half_patch, half_patch)
    patches = jnp.concatenate([blocks[:, :, :-1], blocks[:, :, 1:]], axis=3)
    patches = patches.transpose(1, 2, 0, 3).reshape(PATCH, -1, 2 * PATCH)
    spectrum = jnp.dot(patches, forward_table, preferred_element_type=jnp.float32)
    spec_real = spectrum[..., :PATCH]
    spec_imag = spectrum[..., PATCH:]
    power_spec = spec_real * spec_real + spec_imag * spec_imag
    smooth = power_spec + jnp.roll(power_spec, 1, 0) + jnp.roll(power_spec, -1, 0)
    smooth = smooth + jnp.roll(smooth, 1, 2) + jnp.roll(smooth, -1, 2)
    ref_power = PATCH * PATCH * 1.0
    gain_map = jnp.power((smooth / 9.0 + ref_power) / ref_power, 0.25)
    shaped = jnp.concatenate([spec_real * gain_map, spec_imag * gain_map], axis=-1).astype(jnp.bfloat16)
    range_back = jnp.dot(shaped, inverse_table, preferred_element_type=jnp.float32).astype(jnp.bfloat16)
    range_back = range_back.reshape(PATCH, -1, 2, PATCH)
    lines_back = jnp.einsum('lqcs,cldm->mqds', range_back.astype(jnp.float32), inverse_table.reshape(2, PATCH, 2, PATCH).astype(jnp.float32))
    weighted = lines_back * window[:, None, None, None] * window[None, None, None, :]
    joined = weighted[:, :-1, :, half_patch:] + weighted[:, 1:, :, :half_patch]
    return joined.transpose(2, 0, 1, 3).reshape(2, PATCH, -1)


def filter_item(item_slab, forward_table, inverse_table, window):
    half_patch = PATCH // 2
    width = item_slab.shape[2]
    row_count = item_slab.shape[1] // half_patch - 1

    def single_row(row_index):
        band_rows = lax.dynamic_slice_in_dim(item_slab, row_index * half_patch, PATCH, 1).reshape(2 * PATCH, width)
        return filter_rows(band_rows, forward_table, inverse_table, window)

    row_results = lax.map(single_row, jnp.arange(row_count, dtype=jnp.int32))
    joined = row_results[:-1, :, half_patch:] + row_results[1:, :, :half_patch]
    return joined.transpose(1, 0, 2, 3).reshape(2, (row_count - 1) * half_patch, -1)


def reference(image_stack, tap_weights, offsets, matchings):
    rim_width = SHIFT_MAX + TAPS // 2
    padded = jnp.pad(image_stack, ((0, 0), (0, 0), (rim_width, rim_width), (0, 0)))
    line_ids = jnp.arange(LINES, dtype=jnp.int32)
    summed = jnp.zeros(image_stack.shape, jnp.float32)
    for tap_index in range(TAPS):
        source_rows = (line_ids[None, :] + offsets + (tap_index - (TAPS // 2 - 1) + rim_width)).astype(jnp.int32)
        picked = jax.vmap(lambda slab_one, rows_one: jnp.take(slab_one, rows_one, axis=1), in_axes=(1, 0), out_axes=1)(padded, source_rows)
        summed = summed + tap_weights[tap_index][None, :, :, None] * picked
    resampled = summed.astype(jnp.bfloat16)
    own_real = resampled[0].astype(jnp.float32)
    own_imag = resampled[1].astype(jnp.float32)
    products = []
    for match_index in range(MATCHES):
        partner = jnp.take(resampled, matchings[match_index], axis=1)
        other_real = partner[0].astype(jnp.float32)
        other_imag = partner[1].astype(jnp.float32)
        real_part = own_real * other_real + own_imag * other_imag
        imag_part = own_imag * other_real - own_real * other_imag
        products.append(jnp.stack([real_part, imag_part], axis=0))
    interferogram = jnp.stack(products, axis=0).astype(jnp.bfloat16)
    half_patch = PATCH // 2
    padded_ifg = jnp.pad(interferogram, ((0, 0), (0, 0), (0, 0), (half_patch, half_patch), (half_patch, half_patch)))
    items = padded_ifg.transpose(0, 2, 1, 3, 4).reshape(MATCHES * DATES, 2, LINES + PATCH, SAMPLES + PATCH)
    forward_table = fourier_table(1.0, 1.0)
    inverse_table = fourier_table(-1.0, 1.0 / PATCH)
    window = patch_window()
    results = lax.map(lambda item_slab: filter_item(item_slab, forward_table, inverse_table, window), items)
    return results.reshape(MATCHES, DATES, 2, LINES, SAMPLES).transpose(0, 2, 1, 3, 4)
```

```python
import functools
import math

import jax
import jax.numpy as jnp
import ml_dtypes
import numpy as np
from jax import lax
from jax.experimental import pallas as pl
from jax.experimental.pallas import tpu as pltpu
from jax.sharding import PartitionSpec as P

TAPS = 8
SHIFT_MAX = 12
PATCH = 64
HALF = PATCH // 2
RIM = SHIFT_MAX + TAPS // 2
MESH = pl.DeviceIdType.MESH
BF16 = ml_dtypes.bfloat16
PLACE = {1: 0, 0: 1, -1: 2}


def fourier_table(sine_sign, table_scale):
    ids = np.arange(PATCH)
    angles = ((ids[:, None] * ids[None, :]) % PATCH) * (2.0 * math.pi / PATCH)
    cosine = np.cos(angles) * table_scale
    sine = np.sin(angles) * (sine_sign * table_scale)
    table = np.block([[cosine, -sine], [sine, cosine]]).astype(np.float32)
    return table.astype(BF16).astype(np.float32)


def tables(count):
    forward = fourier_table(1.0, 1.0)
    inverse = fourier_table(-1.0, 1.0 / PATCH)
    window = np.sin(math.pi * (np.arange(PATCH, dtype=np.float32) + 0.5) / PATCH) ** 2
    groups = 3 * count + (3 * count) % 2
    lanes = groups * PATCH
    wide = 2 * PATCH
    line_in = np.zeros((count, 2, wide, 2, groups, PATCH), np.float32)
    line_out = np.zeros((count, 2, PATCH, 2, groups, PATCH), np.float32)
    split_f = forward.reshape(2, PATCH, 2, PATCH)
    split_i = inverse.reshape(2, PATCH, 2, PATCH)
    for j in range(count):
        for r in range(3):
            line_in[j, :, r * HALF : r * HALF + PATCH, :, 3 * j + r] = split_f
            for line in range(PATCH):
                u = line + HALF - HALF * r
                if 0 <= u < PATCH:
                    line_out[j, :, line, :, 3 * j + r] = (
                        split_i[:, :, :, u].transpose(2, 0, 1) * window[u]
                    )
    line_in = line_in.reshape(count * 2 * wide, 2 * lanes).astype(BF16)
    line_out = line_out.reshape(count, 2 * PATCH, 2 * lanes)
    high = line_out.astype(BF16)
    low = (line_out - high.astype(np.float32)).astype(BF16)
    line_out = np.stack([high, low], axis=1).reshape(count * 4 * PATCH, 2 * lanes)
    ids = np.arange(2 * PATCH)
    gap = (ids[:, None] - ids[None, :]) % PATCH
    same = ids[:, None] // PATCH == ids[None, :] // PATCH
    ring = (((gap <= 1) | (gap == PATCH - 1)) & same).astype(BF16)
    window_rows = np.broadcast_to(np.tile(window, 2)[:, None], (2 * PATCH, 128)).astype(np.float32)
    return (
        line_in,
        forward.T.astype(BF16),
        inverse.T.astype(BF16),
        ring,
        line_out,
        np.ascontiguousarray(window_rows),
    )


def exchange_kernel(
    az_size, date_size, image, taps, offsets, out, halo, tile, pack, wide, marg,
    halo_send, halo_recv, send_sem, recv_sem,
):
    a = lax.axis_index("az")
    d = lax.axis_index("date")
    g = lax.axis_index("rg")
    lines = image.shape[2]
    has_up = a > 0
    has_down = a < az_size - 1
    exists = {-1: has_up, 0: None, 1: has_down}

    def guarded(step, body):
        if exists[step] is None:
            body()
        else:
            pl.when(exists[step])(body)

    def place_at(az_step, date_step, other):
        return {
            "az": a + az_step,
            "date": lax.rem(d + date_step, date_size),
            "rg": 1 - g if other else g,
        }

    peers = [
        (o, t, k) for o in (-1, 0, 1) for t in range(date_size) for k in (0, 1)
        if (o, t, k) != (0, 0, 0)
    ]
    barrier = pltpu.get_barrier_semaphore()
    for o, t, k in peers:
        guarded(o, lambda o=o, t=t, k=k: pl.semaphore_signal(
            barrier, inc=1, device_id=place_at(o, t, k), device_id_type=MESH))
    rows_near = 1 + has_up.astype(jnp.int32) + has_down.astype(jnp.int32)
    pl.semaphore_wait(barrier, rows_near * (2 * date_size) - 1)

    def halo_copy(step, target_step):
        first = lines - RIM if step == 1 else 0
        slot = 0 if step == 1 else 1
        return pltpu.make_async_remote_copy(
            src_ref=image.at[:, 0, pl.ds(first, RIM), :],
            dst_ref=halo.at[slot],
            send_sem=halo_send.at[slot],
            recv_sem=halo_recv.at[slot],
            device_id=place_at(target_step, 0, 0),
            device_id_type=MESH,
        )

    for step in (1, -1):
        guarded(step, lambda step=step: halo_copy(step, step).start())

    @pl.when(jnp.logical_not(has_up))
    def _():
        halo[0] = jnp.zeros(halo.shape[1:], halo.dtype)
        wide[:, :, 0:HALF] = jnp.zeros((date_size, 2, HALF, wide.shape[3]), wide.dtype)
        marg[:, 0] = jnp.zeros((date_size,) + marg.shape[2:], marg.dtype)

    @pl.when(jnp.logical_not(has_down))
    def _():
        halo[1] = jnp.zeros(halo.shape[1:], halo.dtype)
        wide[:, :, 3 * HALF :] = jnp.zeros((date_size, 2, HALF, wide.shape[3]), wide.dtype)
        marg[:, 2] = jnp.zeros((date_size,) + marg.shape[2:], marg.dtype)

    span = lines + 2 * RIM
    source = lax.broadcasted_iota(jnp.int32, (span, lines), 0)
    place = lax.broadcasted_iota(jnp.int32, (span, lines), 1)
    gap = source - place - (RIM - (TAPS // 2 - 1)) - offsets[0:1, :]
    band = jnp.zeros((span, lines), jnp.float32)
    for k in range(TAPS):
        band = jnp.where(gap == k, taps[k], band)

    guarded(-1, lambda: halo_copy(1, -1).wait_recv())
    guarded(1, lambda: halo_copy(-1, 1).wait_recv())
    results = []
    for c in range(2):
        stacked = jnp.concatenate([halo[0, c], image[c, 0], halo[1, c]], axis=0)
        results.append(
            lax.dot_general(
                band, stacked, (((0,), (0,)), ((), ())),
                precision=lax.Precision.HIGHEST, preferred_element_type=jnp.float32,
            )
        )
    samples = image.shape[3]
    parts = []
    for c in range(2):
        wide[0, c, HALF : HALF + lines] = results[c].astype(jnp.bfloat16)
        tile[c] = results[c].astype(jnp.bfloat16)
        edge = jnp.where(g == 0, results[c][:, samples - HALF :], results[c][:, :HALF])
        parts += [edge[:HALF], edge[HALF:]]
    pack[...] = jnp.concatenate(parts, axis=1).astype(jnp.bfloat16)

    taken = {1: (HALF, HALF, 0), 0: (0, lines, HALF), -1: (0, HALF, HALF + lines)}

    def tile_copy(o, t, other, target):
        slot = (date_size - t) % date_size
        spot = PLACE[o]
        if other:
            src, dst = pack, marg.at[slot, spot]
        else:
            first, size, land = taken[o]
            src = tile.at[:, pl.ds(first, size), :]
            dst = wide.at[slot, :, pl.ds(land, size), :]
        return pltpu.make_async_remote_copy(
            src_ref=src, dst_ref=dst,
            send_sem=send_sem.at[t, spot, other],
            recv_sem=recv_sem.at[slot, spot, other],
            device_id=target, device_id_type=MESH,
        )

    order = sorted(peers, key=lambda p: (-p[1], abs(p[0]), p[2]))
    for o, t, k in order:
        guarded(o, lambda o=o, t=t, k=k: tile_copy(o, t, k, place_at(o, t, k)).start())
    for o, t, k in order:
        guarded(-o, lambda o=o, t=t, k=k: tile_copy(
            o, t, k, place_at(-o, (date_size - t) % date_size, k)).wait_recv())

    blank = jnp.zeros((4 * HALF, out.shape[3] - samples - HALF), jnp.bfloat16)
    for t in range(date_size):
        for c in range(2):
            blocks = [
                marg[t, spot][:, (2 * c + h) * HALF : (2 * c + h + 1) * HALF].astype(jnp.float32)
                for spot, h in ((0, 1), (1, 0), (1, 1), (2, 0))
            ]
            side = jnp.concatenate(blocks, axis=0).astype(jnp.bfloat16)
            out[t, c, :, 0:samples] = wide[t, c]
            out[t, c, :, samples:] = jnp.concatenate([side, blank], axis=1)

    for step in (1, -1):
        guarded(step, lambda step=step: halo_copy(step, step).wait_send())
    for o, t, k in order:
        guarded(o, lambda o=o, t=t, k=k: tile_copy(o, t, k, place_at(o, t, k)).wait_send())


def filter_kernel(
    date_size, count, matchings, wide, line_in, forward, inverse, ring, line_out, window,
    out, back,
):
    d = lax.axis_index("date")
    g = lax.axis_index("rg")
    matches = out.shape[0]
    samples = out.shape[4]
    lanes = line_in.shape[1] // 2
    wanted = [
        lax.rem(matchings[m, d] - d + date_size, date_size) for m in range(matches)
    ]

    def turned(slab):
        rows = jnp.concatenate([slab[0], slab[1]], axis=0).astype(jnp.float32)
        flipped = rows.T
        core, side = flipped[:samples], flipped[samples : samples + HALF]
        zero = jnp.zeros_like(side)
        left = jnp.where(g == 0, zero, side)
        right = jnp.where(g == 0, side, zero)
        return jnp.concatenate([left, core, right], axis=0)

    own = turned(wide[0])
    own_real, own_imag = own[:, : 2 * PATCH], own[:, 2 * PATCH :]
    pieces = []
    for j in range(count):
        if count == date_size:
            other = own if j == 0 else turned(wide[j])
        else:
            other = turned(wide[wanted[j]])
        other_real, other_imag = other[:, : 2 * PATCH], other[:, 2 * PATCH :]
        pieces.append(own_real * other_real + own_imag * other_imag)
        pieces.append(own_imag * other_real - own_real * other_imag)
    ifg = jnp.concatenate(pieces, axis=1).astype(jnp.bfloat16)
    spectra = jnp.dot(ifg, line_in[...], preferred_element_type=jnp.float32).astype(jnp.bfloat16)

    ref_power = PATCH * PATCH * 1.0
    weights = jnp.concatenate([window[...]] * (lanes // 128), axis=1)
    held = None
    for q in range(samples // HALF + 1):
        rows = spectra[q * HALF : q * HALF + PATCH]
        block = jnp.concatenate([rows[:, :lanes], rows[:, lanes:]], axis=0)
        spectrum = jnp.dot(forward[...], block, preferred_element_type=jnp.float32)
        real, imag = spectrum[:PATCH], spectrum[PATCH:]
        power = real * real + imag * imag
        summed = power + pltpu.roll(power, 1, 0) + pltpu.roll(power, PATCH - 1, 0)
        summed = summed.astype(jnp.bfloat16)
        tiles = jnp.concatenate(
            [summed[:, i * 128 : (i + 1) * 128] for i in range(lanes // 128)], axis=0
        )
        smooth = jnp.dot(tiles, ring[...], preferred_element_type=jnp.float32)
        gain = lax.rsqrt(lax.rsqrt(1.0 + smooth * (1.0 / (9.0 * ref_power))))
        gain = jnp.concatenate(
            [gain[i * PATCH : (i + 1) * PATCH] for i in range(lanes // 128)], axis=1
        )
        shaped = jnp.concatenate([real * gain, imag * gain], axis=0).astype(jnp.bfloat16)
        ranged = jnp.dot(inverse[...], shaped, preferred_element_type=jnp.float32) * weights
        if held is not None:
            for c in range(2):
                joined = held[c] + ranged[c * PATCH : c * PATCH + HALF]
                back[(q - 1) * HALF : q * HALF, c * lanes : (c + 1) * lanes] = joined.astype(
                    jnp.bfloat16
                )
        held = [ranged[c * PATCH + HALF : (c + 1) * PATCH] for c in range(2)]

    result = lax.dot_general(
        line_out[...], back[...], (((1,), (1,)), ((), ())), preferred_element_type=jnp.float32
    )
    for j in range(count):
        first = result[j * 4 * PATCH : j * 4 * PATCH + 2 * PATCH]
        second = result[j * 4 * PATCH + 2 * PATCH : (j + 1) * 4 * PATCH]
        joined = first + second

        def keep(m, joined=joined):
            out[m, 0, 0] = joined[:PATCH]
            out[m, 1, 0] = joined[PATCH:]

        if count == date_size:
            for m in range(matches):
                pl.when(wanted[m] == j)(functools.partial(keep, m))
        else:
            keep(j)


def per_device(az_size, date_size, image_stack, tap_weights, offsets, matchings):
    lines, samples = image_stack.shape[2:]
    assert image_stack.shape[1] == 1 and lines == PATCH
    matches = matchings.shape[0]
    vmem = pl.BlockSpec(memory_space=pltpu.VMEM)
    smem = pl.BlockSpec(memory_space=pltpu.SMEM)
    wide = pl.pallas_call(
        functools.partial(exchange_kernel, az_size, date_size),
        out_shape=jax.ShapeDtypeStruct((date_size, 2, 4 * HALF, samples + 128), jnp.bfloat16),
        in_specs=[vmem] * 3,
        out_specs=vmem,
        scratch_shapes=[
            pltpu.VMEM((2, 2, RIM, samples), jnp.float32),
            pltpu.VMEM((2, lines, samples), jnp.bfloat16),
            pltpu.VMEM((HALF, 4 * HALF), jnp.bfloat16),
            pltpu.VMEM((date_size, 2, 4 * HALF, samples), jnp.bfloat16),
            pltpu.VMEM((date_size, 3, HALF, 4 * HALF), jnp.bfloat16),
            pltpu.SemaphoreType.DMA((2,)),
            pltpu.SemaphoreType.DMA((2,)),
            pltpu.SemaphoreType.DMA((date_size, 3, 2)),
            pltpu.SemaphoreType.DMA((date_size, 3, 2)),
        ],
        compiler_params=pltpu.CompilerParams(collective_id=0, has_side_effects=True),
    )(image_stack, tap_weights, offsets)
    count = min(matches, date_size)
    constants = tables(count)
    lanes = constants[0].shape[1] // 2
    return pl.pallas_call(
        functools.partial(filter_kernel, date_size, count),
        out_shape=jax.ShapeDtypeStruct((matches, 2, 1, lines, samples), jnp.float32),
        in_specs=[smem] + [vmem] * 7,
        out_specs=vmem,
        scratch_shapes=[pltpu.VMEM((samples, 2 * lanes), jnp.bfloat16)],
    )(matchings, wide, *[jnp.asarray(c) for c in constants])


def solution(mesh):
    placed = (
        P(None, ("parts", "date"), "az", "rg"),
        P(None, ("parts", "date"), "az"),
        P(("parts", "date"), "az"),
        P(),
    )
    assert mesh.shape["rg"] == 2
    return jax.shard_map(
        functools.partial(per_device, mesh.shape["az"], mesh.shape["date"]),
        mesh=mesh,
        in_specs=placed,
        out_specs=P(None, None, ("parts", "date"), "az", "rg"),
        check_vma=False,
    )
```

```python
import functools
import math

import jax
import jax.numpy as jnp
import ml_dtypes
import numpy as np
from jax import lax
from jax.experimental import pallas as pl
from jax.experimental.pallas import tpu as pltpu
from jax.sharding import PartitionSpec as P

TAPS = 8
SHIFT_MAX = 12
PATCH = 64
HALF = PATCH // 2
RIM = SHIFT_MAX + TAPS // 2
GROUPS = 4
LANES = GROUPS * PATCH
MESH = pl.DeviceIdType.MESH
BF16 = ml_dtypes.bfloat16
PLACE = {1: 0, 0: 1, -1: 2}


def fourier_table(sine_sign, table_scale):
    ids = np.arange(PATCH)
    angles = ((ids[:, None] * ids[None, :]) % PATCH) * (2.0 * math.pi / PATCH)
    cosine = np.cos(angles) * table_scale
    sine = np.sin(angles) * (sine_sign * table_scale)
    table = np.block([[cosine, -sine], [sine, cosine]]).astype(np.float32)
    return table.astype(BF16).astype(np.float32)


def tables():
    forward = fourier_table(1.0, 1.0)
    inverse = fourier_table(-1.0, 1.0 / PATCH)
    window = np.sin(math.pi * (np.arange(PATCH, dtype=np.float32) + 0.5) / PATCH) ** 2
    wide = 2 * PATCH
    line_in = np.zeros((2, wide, 2, GROUPS, PATCH), np.float32)
    line_out = np.zeros((2, PATCH, 2, GROUPS, PATCH), np.float32)
    split_f = forward.reshape(2, PATCH, 2, PATCH)
    split_i = inverse.reshape(2, PATCH, 2, PATCH)
    for r in range(3):
        line_in[:, r * HALF : r * HALF + PATCH, :, r] = split_f
        for line in range(PATCH):
            u = line + HALF - HALF * r
            if 0 <= u < PATCH:
                line_out[:, line, :, r] = split_i[:, :, :, u].transpose(2, 0, 1) * window[u]
    line_in = line_in.reshape(2 * wide, 2 * LANES).astype(BF16)
    line_out = line_out.reshape(wide, 2 * LANES)
    high = line_out.astype(BF16)
    low = (line_out - high.astype(np.float32)).astype(BF16)
    ids = np.arange(LANES)
    gap = (ids[:, None] - ids[None, :]) % PATCH
    same = ids[:, None] // PATCH == ids[None, :] // PATCH
    ring = (((gap <= 1) | (gap == PATCH - 1)) & same).astype(BF16)
    turns = np.concatenate([forward.T, inverse.T], axis=0).astype(BF16)
    rows = np.broadcast_to(np.tile(window, 2)[:, None], (wide, wide)).astype(np.float32)
    rows_high = rows.astype(BF16)
    rows_low = (rows - rows_high.astype(np.float32)).astype(BF16)
    last = np.concatenate([ring, turns, np.concatenate([rows_high, rows_low], axis=0)], axis=1)
    return np.concatenate([line_in, high, low, last], axis=0)


def stack_kernel(
    az_size, date_size, count, image_hbm, taps_hbm, offsets_hbm, table_hbm, *rest,
):
    if count < date_size:
        matchings, *rest = rest
    (
        out, image, taps, offsets, table, halo, tile, pack, wide, marg, spec, power_sum, shaped,
        back, load_sem, halo_send, halo_recv, send_sem, recv_sem,
    ) = rest
    a = lax.axis_index("az")
    d = lax.axis_index("date")
    g = lax.axis_index("rg")
    lines = image.shape[2]
    samples = image.shape[3]
    loads = [
        pltpu.make_async_copy(source, target, load_sem.at[i])
        for i, (source, target) in enumerate(
            ((offsets_hbm, offsets), (taps_hbm, taps), (image_hbm, image), (table_hbm, table))
        )
    ]
    has_up = a > 0
    has_down = a < az_size - 1
    exists = {-1: has_up, 0: None, 1: has_down}

    def guarded(step, body):
        if exists[step] is None:
            body()
        else:
            pl.when(exists[step])(body)

    def place_at(az_step, date_step, other):
        return {
            "az": a + az_step,
            "date": lax.rem(d + date_step, date_size),
            "rg": 1 - g if other else g,
        }

    peers = [
        (o, t, k) for o in (-1, 0, 1) for t in range(date_size) for k in (0, 1)
        if (o, t, k) != (0, 0, 0)
    ]
    barrier = pltpu.get_barrier_semaphore()
    for o, t, k in peers:
        guarded(o, lambda o=o, t=t, k=k: pl.semaphore_signal(
            barrier, inc=1, device_id=place_at(o, t, k), device_id_type=MESH))
    for load in loads:
        load.start()
    rows_near = 1 + has_up.astype(jnp.int32) + has_down.astype(jnp.int32)
    pl.semaphore_wait(barrier, rows_near * (2 * date_size) - 1)

    def halo_copy(step, target_step):
        first = lines - RIM if step == 1 else 0
        slot = 0 if step == 1 else 1
        return pltpu.make_async_remote_copy(
            src_ref=image_hbm.at[:, 0, pl.ds(first, RIM), :],
            dst_ref=halo.at[slot],
            send_sem=halo_send.at[slot],
            recv_sem=halo_recv.at[slot],
            device_id=place_at(target_step, 0, 0),
            device_id_type=MESH,
        )

    for step in (1, -1):
        guarded(step, lambda step=step: halo_copy(step, step).start())

    @pl.when(jnp.logical_not(has_up))
    def _():
        halo[0] = jnp.zeros(halo.shape[1:], halo.dtype)
        wide[:, :, 0:HALF] = jnp.zeros((date_size, 2, HALF, wide.shape[3]), wide.dtype)
        marg[:, 0] = jnp.zeros((date_size,) + marg.shape[2:], marg.dtype)

    @pl.when(jnp.logical_not(has_down))
    def _():
        halo[1] = jnp.zeros(halo.shape[1:], halo.dtype)
        wide[:, :, 3 * HALF :] = jnp.zeros((date_size, 2, HALF, wide.shape[3]), wide.dtype)
        marg[:, 2] = jnp.zeros((date_size,) + marg.shape[2:], marg.dtype)

    for load in loads[:3]:
        load.wait()
    span = lines + 2 * RIM
    source = lax.broadcasted_iota(jnp.int32, (span, lines), 0)
    place = lax.broadcasted_iota(jnp.int32, (span, lines), 1)
    gap = source - place - (RIM - (TAPS // 2 - 1)) - offsets[0:1, :]
    band = jnp.zeros((span, lines), jnp.float32)
    for k in range(TAPS):
        band = jnp.where(gap == k, taps[k], band)

    guarded(-1, lambda: halo_copy(1, -1).wait_recv())
    guarded(1, lambda: halo_copy(-1, 1).wait_recv())
    stacked = jnp.concatenate(
        [
            jnp.concatenate([halo[0, c], image[c, 0], halo[1, c]], axis=0)
            for c in range(2)
        ],
        axis=1,
    )
    both = lax.dot_general(
        band, stacked, (((0,), (0,)), ((), ())),
        precision=lax.Precision.HIGHEST, preferred_element_type=jnp.float32,
    )
    results = [both[:, :samples], both[:, samples:]]
    parts = []
    for c in range(2):
        wide[0, c, HALF : HALF + lines] = results[c].astype(jnp.bfloat16)
        tile[c] = results[c].astype(jnp.bfloat16)
        edge = jnp.where(g == 0, results[c][:, samples - HALF :], results[c][:, :HALF])
        parts += [edge[:HALF], edge[HALF:]]
    pack[...] = jnp.concatenate(parts, axis=1).astype(jnp.bfloat16)

    taken = {1: (HALF, HALF, 0), 0: (0, lines, HALF), -1: (0, HALF, HALF + lines)}

    def tile_copy(o, t, other, target):
        slot = (date_size - t) % date_size
        spot = PLACE[o]
        if other:
            src, dst = pack, marg.at[slot, spot]
        else:
            first, size, land = taken[o]
            src = tile.at[:, pl.ds(first, size), :]
            dst = wide.at[slot, :, pl.ds(land, size), :]
        return pltpu.make_async_remote_copy(
            src_ref=src, dst_ref=dst,
            send_sem=send_sem.at[t, spot, other],
            recv_sem=recv_sem.at[slot, spot, other],
            device_id=target, device_id_type=MESH,
        )

    order = sorted(peers, key=lambda p: (p[1], abs(p[0]), p[2]))
    for o, t, k in order:
        guarded(o, lambda o=o, t=t, k=k: tile_copy(o, t, k, place_at(o, t, k)).start())

    def arrived(slot):
        for o, t, k in order:
            if (date_size - t) % date_size == slot:
                guarded(-o, lambda o=o, t=t, k=k: tile_copy(
                    o, t, k, place_at(-o, slot, k)).wait_recv())

    def turned(slot):
        core = jnp.concatenate([wide[slot, 0], wide[slot, 1]], axis=0).astype(jnp.float32).T
        blocks = []
        for c in range(2):
            for spot, h in ((0, 1), (1, 0), (1, 1), (2, 0)):
                first = (2 * c + h) * HALF
                blocks.append(marg[slot, spot][:, first : first + HALF].astype(jnp.float32))
        side = jnp.concatenate(blocks, axis=0)
        side = jnp.concatenate([side, jnp.zeros((side.shape[0], 128 - HALF), jnp.float32)], axis=1)
        side = side.T[:HALF]
        zero = jnp.zeros_like(side)
        left = jnp.where(g == 0, zero, side)
        right = jnp.where(g == 0, side, zero)
        return jnp.concatenate([left, core, right], axis=0)

    def filtered(own, other):
        wide_lines = 2 * PATCH
        own_real, own_imag = own[:, :wide_lines], own[:, wide_lines:]
        other_real, other_imag = other[:, :wide_lines], other[:, wide_lines:]
        real_part = own_real * other_real + own_imag * other_imag
        imag_part = own_imag * other_real - own_real * other_imag
        ifg = jnp.concatenate([real_part, imag_part], axis=1).astype(jnp.bfloat16)
        spectra = jnp.dot(
            ifg, table[0 : 2 * wide_lines], preferred_element_type=jnp.float32
        ).astype(jnp.bfloat16)
        ring = table[4 * wide_lines :, 0:LANES]
        forward = table[4 * wide_lines : 5 * wide_lines, LANES : LANES + wide_lines]
        inverse = table[5 * wide_lines :, LANES : LANES + wide_lines]
        rows = [
            table[i * wide_lines : (i + 1) * wide_lines, LANES + wide_lines :].astype(jnp.float32)
            for i in (4, 5)
        ]
        weights = rows[0] + rows[1]
        weights = jnp.concatenate([weights] * (LANES // wide_lines), axis=1)
        columns = samples // HALF + 1
        for q in range(columns):
            rows = spectra[q * HALF : q * HALF + PATCH]
            block = jnp.concatenate([rows[:, :LANES], rows[:, LANES:]], axis=0)
            spectrum = jnp.dot(forward, block, preferred_element_type=jnp.float32)
            spec[q] = spectrum
            real, imag = spectrum[:PATCH], spectrum[PATCH:]
            power = real * real + imag * imag
            summed = power + pltpu.roll(power, 1, 0) + pltpu.roll(power, PATCH - 1, 0)
            power_sum[q * PATCH : (q + 1) * PATCH] = summed.astype(jnp.bfloat16)
        smooth = jnp.dot(power_sum[...], ring, preferred_element_type=jnp.float32)
        gains = lax.rsqrt(lax.rsqrt(1.0 + smooth * (1.0 / (9.0 * PATCH * PATCH))))
        for q in range(columns):
            gain = gains[q * PATCH : (q + 1) * PATCH]
            shaped[q, :PATCH] = (spec[q, :PATCH] * gain).astype(jnp.bfloat16)
            shaped[q, PATCH:] = (spec[q, PATCH:] * gain).astype(jnp.bfloat16)
        held = None
        for q in range(columns):
            ranged = jnp.dot(inverse, shaped[q], preferred_element_type=jnp.float32) * weights
            if held is not None:
                for c in range(2):
                    joined = held[c] + ranged[c * PATCH : c * PATCH + HALF]
                    back[(q - 1) * HALF : q * HALF, c * LANES : (c + 1) * LANES] = joined.astype(
                        jnp.bfloat16
                    )
            held = [ranged[c * PATCH + HALF : (c + 1) * PATCH] for c in range(2)]
        split = lax.dot_general(
            table[2 * wide_lines : 4 * wide_lines], back[...], (((1,), (1,)), ((), ())),
            preferred_element_type=jnp.float32,
        )
        return split[:wide_lines] + split[wide_lines:]

    loads[3].wait()
    arrived(0)
    own = turned(0)
    if count == date_size:
        for j in range(count):
            if j:
                arrived(j)
            out[j] = filtered(own, turned(j) if j else own)
    else:
        for j in range(1, date_size):
            arrived(j)
        for m in range(count):
            slot = lax.rem(matchings[d, m] - d + date_size, date_size)
            out[m] = filtered(own, turned(slot))

    for step in (1, -1):
        guarded(step, lambda step=step: halo_copy(step, step).wait_send())
    for o, t, k in order:
        guarded(o, lambda o=o, t=t, k=k: tile_copy(o, t, k, place_at(o, t, k)).wait_send())


def spread_kernel(date_size, count, matchings, results, out, sem):
    d = lax.axis_index("date")
    copies = []
    for m in range(out.shape[0]):
        spot = m
        if count == date_size:
            spot = lax.rem(matchings[d, m] - d + date_size, date_size)
        for c in range(2):
            copies.append(
                pltpu.make_async_copy(
                    results.at[spot, pl.ds(c * PATCH, PATCH)], out.at[m, c, 0], sem.at[m, c]
                )
            )
    for copy in copies:
        copy.start()
    for copy in copies:
        copy.wait()


def per_device(az_size, date_size, image_stack, tap_weights, offsets, matchings):
    lines, samples = image_stack.shape[2:]
    assert image_stack.shape[1] == 1 and lines == PATCH
    matches = matchings.shape[0]
    count = min(matches, date_size)
    columns = samples // HALF + 1
    by_date = matchings.T
    hbm = pl.BlockSpec(memory_space=pl.ANY)
    vmem = pl.BlockSpec(memory_space=pltpu.VMEM)
    smem = pl.BlockSpec(memory_space=pltpu.SMEM)
    constants = tables()
    extra = [by_date] if count < date_size else []
    results = pl.pallas_call(
        functools.partial(stack_kernel, az_size, date_size, count),
        out_shape=jax.ShapeDtypeStruct((count, 2 * lines, samples), jnp.float32),
        in_specs=[hbm] * 4 + [smem] * len(extra),
        out_specs=vmem,
        scratch_shapes=[
            pltpu.VMEM(image_stack.shape, jnp.float32),
            pltpu.VMEM(tap_weights.shape, jnp.float32),
            pltpu.VMEM(offsets.shape, jnp.int32),
            pltpu.VMEM(constants.shape, jnp.bfloat16),
            pltpu.VMEM((2, 2, RIM, samples), jnp.float32),
            pltpu.VMEM((2, lines, samples), jnp.bfloat16),
            pltpu.VMEM((HALF, 4 * HALF), jnp.bfloat16),
            pltpu.VMEM((date_size, 2, 4 * HALF, samples), jnp.bfloat16),
            pltpu.VMEM((date_size, 3, HALF, 4 * HALF), jnp.bfloat16),
            pltpu.VMEM((columns, 2 * PATCH, LANES), jnp.float32),
            pltpu.VMEM((columns * PATCH, LANES), jnp.bfloat16),
            pltpu.VMEM((columns, 2 * PATCH, LANES), jnp.bfloat16),
            pltpu.VMEM((samples, 2 * LANES), jnp.bfloat16),
            pltpu.SemaphoreType.DMA((4,)),
            pltpu.SemaphoreType.DMA((2,)),
            pltpu.SemaphoreType.DMA((2,)),
            pltpu.SemaphoreType.DMA((date_size, 3, 2)),
            pltpu.SemaphoreType.DMA((date_size, 3, 2)),
        ],
        compiler_params=pltpu.CompilerParams(collective_id=0, has_side_effects=True),
    )(image_stack, tap_weights, offsets, jnp.asarray(constants), *extra)
    return pl.pallas_call(
        functools.partial(spread_kernel, date_size, count),
        out_shape=jax.ShapeDtypeStruct((matches, 2, 1, lines, samples), jnp.float32),
        in_specs=[smem, hbm],
        out_specs=hbm,
        scratch_shapes=[pltpu.SemaphoreType.DMA((matches, 2))],
    )(by_date, results)


def solution(mesh):
    placed = (
        P(None, ("parts", "date"), "az", "rg"),
        P(None, ("parts", "date"), "az"),
        P(("parts", "date"), "az"),
        P(),
    )
    assert mesh.shape["rg"] == 2
    return jax.shard_map(
        functools.partial(per_device, mesh.shape["az"], mesh.shape["date"]),
        mesh=mesh,
        in_specs=placed,
        out_specs=P(None, None, ("parts", "date"), "az", "rg"),
        check_vma=False,
    )
```

```python
import functools
import math

import jax
import jax.numpy as jnp
import ml_dtypes
import numpy as np
from jax import lax
from jax.experimental import pallas as pl
from jax.experimental.pallas import tpu as pltpu
from jax.sharding import PartitionSpec as P

TAPS = 8
SHIFT_MAX = 12
PATCH = 64
HALF = PATCH // 2
RIM = SHIFT_MAX + TAPS // 2
GROUPS = 4
LANES = GROUPS * PATCH
VMEM_LIMIT = 24 << 20
MESH = pl.DeviceIdType.MESH
BF16 = ml_dtypes.bfloat16
PLACE = {1: 0, 0: 1, -1: 2}


def fourier_table(sine_sign, table_scale):
    ids = np.arange(PATCH)
    angles = ((ids[:, None] * ids[None, :]) % PATCH) * (2.0 * math.pi / PATCH)
    cosine = np.cos(angles) * table_scale
    sine = np.sin(angles) * (sine_sign * table_scale)
    table = np.block([[cosine, -sine], [sine, cosine]]).astype(np.float32)
    return table.astype(BF16).astype(np.float32)


def tables():
    forward = fourier_table(1.0, 1.0)
    inverse = fourier_table(-1.0, 1.0 / PATCH)
    window = np.sin(math.pi * (np.arange(PATCH, dtype=np.float32) + 0.5) / PATCH) ** 2
    wide = 2 * PATCH
    line_in = np.zeros((2, wide, 2, GROUPS, PATCH), np.float32)
    line_out = np.zeros((2, PATCH, 2, GROUPS, PATCH), np.float32)
    split_f = forward.reshape(2, PATCH, 2, PATCH)
    split_i = inverse.reshape(2, PATCH, 2, PATCH)
    for r in range(3):
        line_in[:, r * HALF : r * HALF + PATCH, :, r] = split_f
        for line in range(PATCH):
            u = line + HALF - HALF * r
            if 0 <= u < PATCH:
                line_out[:, line, :, r] = split_i[:, :, :, u].transpose(2, 0, 1) * window[u]
    line_in = line_in.reshape(2 * wide, 2 * LANES).astype(BF16)
    line_out = line_out.reshape(wide, 2 * LANES)
    high = line_out.astype(BF16)
    low = (line_out - high.astype(np.float32)).astype(BF16)
    ids = np.arange(LANES)
    gap = (ids[:, None] - ids[None, :]) % PATCH
    same = ids[:, None] // PATCH == ids[None, :] // PATCH
    ring = (((gap <= 1) | (gap == PATCH - 1)) & same).astype(BF16)
    turns = np.concatenate([forward.T, inverse.T], axis=0).astype(BF16)
    rows = np.broadcast_to(np.tile(window, 2)[:, None], (wide, wide)).astype(np.float32)
    rows_high = rows.astype(BF16)
    rows_low = (rows - rows_high.astype(np.float32)).astype(BF16)
    last = np.concatenate([ring, turns, np.concatenate([rows_high, rows_low], axis=0)], axis=1)
    return np.concatenate([line_in, high, low, last], axis=0)


def stack_kernel(
    az_size, date_size, count, image_hbm, taps_hbm, offsets_hbm, table_hbm, *rest,
):
    if count < date_size:
        matchings, *rest = rest
    (
        out, image, taps, offsets, table, halo, tile, pack, wide, marg, spec, power_sum, shaped,
        back, load_sem, halo_send, halo_recv, send_sem, recv_sem,
    ) = rest
    a = lax.axis_index("az")
    d = lax.axis_index("date")
    g = lax.axis_index("rg")
    lines = image.shape[2]
    samples = image.shape[3]
    loads = [
        pltpu.make_async_copy(source, target, load_sem.at[i])
        for i, (source, target) in enumerate(
            ((offsets_hbm, offsets), (taps_hbm, taps), (image_hbm, image), (table_hbm, table))
        )
    ]
    has_up = a > 0
    has_down = a < az_size - 1
    exists = {-1: has_up, 0: None, 1: has_down}

    def guarded(step, body):
        if exists[step] is None:
            body()
        else:
            pl.when(exists[step])(body)

    def place_at(az_step, date_step, other):
        return {
            "az": a + az_step,
            "date": lax.rem(d + date_step, date_size),
            "rg": 1 - g if other else g,
        }

    peers = [
        (o, t, k) for o in (-1, 0, 1) for t in range(date_size) for k in (0, 1)
        if (o, t, k) != (0, 0, 0)
    ]
    barrier = pltpu.get_barrier_semaphore()
    for o, t, k in peers:
        guarded(o, lambda o=o, t=t, k=k: pl.semaphore_signal(
            barrier, inc=1, device_id=place_at(o, t, k), device_id_type=MESH))
    for load in loads:
        load.start()
    rows_near = 1 + has_up.astype(jnp.int32) + has_down.astype(jnp.int32)
    pl.semaphore_wait(barrier, rows_near * (2 * date_size) - 1)

    def halo_copy(step, target_step):
        first = lines - RIM if step == 1 else 0
        slot = 0 if step == 1 else 1
        return pltpu.make_async_remote_copy(
            src_ref=image_hbm.at[:, 0, pl.ds(first, RIM), :],
            dst_ref=halo.at[slot],
            send_sem=halo_send.at[slot],
            recv_sem=halo_recv.at[slot],
            device_id=place_at(target_step, 0, 0),
            device_id_type=MESH,
        )

    for step in (1, -1):
        guarded(step, lambda step=step: halo_copy(step, step).start())

    @pl.when(jnp.logical_not(has_up))
    def _():
        halo[0] = jnp.zeros(halo.shape[1:], halo.dtype)
        wide[:, :, 0:HALF] = jnp.zeros((date_size, 2, HALF, wide.shape[3]), wide.dtype)
        marg[:, 0] = jnp.zeros((date_size,) + marg.shape[2:], marg.dtype)

    @pl.when(jnp.logical_not(has_down))
    def _():
        halo[1] = jnp.zeros(halo.shape[1:], halo.dtype)
        wide[:, :, 3 * HALF :] = jnp.zeros((date_size, 2, HALF, wide.shape[3]), wide.dtype)
        marg[:, 2] = jnp.zeros((date_size,) + marg.shape[2:], marg.dtype)

    for load in loads[:3]:
        load.wait()
    span = lines + 2 * RIM
    source = lax.broadcasted_iota(jnp.int32, (span, lines), 0)
    place = lax.broadcasted_iota(jnp.int32, (span, lines), 1)
    gap = source - place - (RIM - (TAPS // 2 - 1)) - offsets[0:1, :]
    band = jnp.zeros((span, lines), jnp.float32)
    for k in range(TAPS):
        band = jnp.where(gap == k, taps[k], band)

    guarded(-1, lambda: halo_copy(1, -1).wait_recv())
    guarded(1, lambda: halo_copy(-1, 1).wait_recv())
    stacked = jnp.concatenate(
        [
            jnp.concatenate([halo[0, c], image[c, 0], halo[1, c]], axis=0)
            for c in range(2)
        ],
        axis=1,
    )
    both = lax.dot_general(
        band, stacked, (((0,), (0,)), ((), ())),
        precision=lax.Precision.HIGHEST, preferred_element_type=jnp.float32,
    )
    results = [both[:, :samples], both[:, samples:]]
    parts = []
    for c in range(2):
        wide[0, c, HALF : HALF + lines] = results[c].astype(jnp.bfloat16)
        tile[c] = results[c].astype(jnp.bfloat16)
        edge = jnp.where(g == 0, results[c][:, samples - HALF :], results[c][:, :HALF])
        parts += [edge[:HALF], edge[HALF:]]
    pack[...] = jnp.concatenate(parts, axis=1).astype(jnp.bfloat16)

    taken = {1: (HALF, HALF, 0), 0: (0, lines, HALF), -1: (0, HALF, HALF + lines)}

    def tile_copy(o, t, other, target):
        slot = (date_size - t) % date_size
        spot = PLACE[o]
        if other:
            src, dst = pack, marg.at[slot, spot]
        else:
            first, size, land = taken[o]
            src = tile.at[:, pl.ds(first, size), :]
            dst = wide.at[slot, :, pl.ds(land, size), :]
        return pltpu.make_async_remote_copy(
            src_ref=src, dst_ref=dst,
            send_sem=send_sem.at[t, spot, other],
            recv_sem=recv_sem.at[slot, spot, other],
            device_id=target, device_id_type=MESH,
        )

    order = sorted(peers, key=lambda p: (p[1], abs(p[0]), p[2]))
    for o, t, k in order:
        guarded(o, lambda o=o, t=t, k=k: tile_copy(o, t, k, place_at(o, t, k)).start())

    def arrived(slot):
        for o, t, k in order:
            if (date_size - t) % date_size == slot:
                guarded(-o, lambda o=o, t=t, k=k: tile_copy(
                    o, t, k, place_at(-o, slot, k)).wait_recv())

    def turned(slot):
        core = jnp.concatenate([wide[slot, 0], wide[slot, 1]], axis=0).astype(jnp.float32).T
        blocks = []
        for c in range(2):
            for spot, h in ((0, 1), (1, 0), (1, 1), (2, 0)):
                first = (2 * c + h) * HALF
                blocks.append(marg[slot, spot][:, first : first + HALF].astype(jnp.float32))
        side = jnp.concatenate(blocks, axis=0)
        side = jnp.concatenate([side, jnp.zeros((side.shape[0], 128 - HALF), jnp.float32)], axis=1)
        side = side.T[:HALF]
        zero = jnp.zeros_like(side)
        left = jnp.where(g == 0, zero, side)
        right = jnp.where(g == 0, side, zero)
        return jnp.concatenate([left, core, right], axis=0)

    def filtered(own, other):
        wide_lines = 2 * PATCH
        own_real, own_imag = own[:, :wide_lines], own[:, wide_lines:]
        other_real, other_imag = other[:, :wide_lines], other[:, wide_lines:]
        real_part = own_real * other_real + own_imag * other_imag
        imag_part = own_imag * other_real - own_real * other_imag
        ifg = jnp.concatenate([real_part, imag_part], axis=1).astype(jnp.bfloat16)
        spectra = jnp.dot(
            ifg, table[0 : 2 * wide_lines], preferred_element_type=jnp.float32
        ).astype(jnp.bfloat16)
        ring = table[4 * wide_lines :, 0:LANES]
        forward = table[4 * wide_lines : 5 * wide_lines, LANES : LANES + wide_lines]
        inverse = table[5 * wide_lines :, LANES : LANES + wide_lines]
        rows = [
            table[i * wide_lines : (i + 1) * wide_lines, LANES + wide_lines :].astype(jnp.float32)
            for i in (4, 5)
        ]
        weights = rows[0] + rows[1]
        weights = jnp.concatenate([weights] * (LANES // wide_lines), axis=1)
        columns = samples // HALF + 1
        for q in range(columns):
            rows = spectra[q * HALF : q * HALF + PATCH]
            block = jnp.concatenate([rows[:, :LANES], rows[:, LANES:]], axis=0)
            spectrum = jnp.dot(forward, block, preferred_element_type=jnp.float32)
            spec[q] = spectrum
            real, imag = spectrum[:PATCH], spectrum[PATCH:]
            power = real * real + imag * imag
            summed = power + pltpu.roll(power, 1, 0) + pltpu.roll(power, PATCH - 1, 0)
            power_sum[q * PATCH : (q + 1) * PATCH] = summed.astype(jnp.bfloat16)
        smooth = jnp.dot(power_sum[...], ring, preferred_element_type=jnp.float32)
        gains = lax.rsqrt(lax.rsqrt(1.0 + smooth * (1.0 / (9.0 * PATCH * PATCH))))
        for q in range(columns):
            gain = gains[q * PATCH : (q + 1) * PATCH]
            shaped[q, :PATCH] = (spec[q, :PATCH] * gain).astype(jnp.bfloat16)
            shaped[q, PATCH:] = (spec[q, PATCH:] * gain).astype(jnp.bfloat16)
        held = None
        for q in range(columns):
            ranged = jnp.dot(inverse, shaped[q], preferred_element_type=jnp.float32) * weights
            if held is not None:
                for c in range(2):
                    joined = held[c] + ranged[c * PATCH : c * PATCH + HALF]
                    back[(q - 1) * HALF : q * HALF, c * LANES : (c + 1) * LANES] = joined.astype(
                        jnp.bfloat16
                    )
            held = [ranged[c * PATCH + HALF : (c + 1) * PATCH] for c in range(2)]
        split = lax.dot_general(
            table[2 * wide_lines : 4 * wide_lines], back[...], (((1,), (1,)), ((), ())),
            preferred_element_type=jnp.float32,
        )
        return split[:wide_lines] + split[wide_lines:]

    loads[3].wait()
    arrived(0)
    own = turned(0)
    if count == date_size:
        for j in range(count):
            if j:
                arrived(j)
            out[j] = filtered(own, turned(j) if j else own)
    else:
        for j in range(1, date_size):
            arrived(j)
        for m in range(count):
            slot = lax.rem(matchings[d, m] - d + date_size, date_size)
            out[m] = filtered(own, turned(slot))

    for step in (1, -1):
        guarded(step, lambda step=step: halo_copy(step, step).wait_send())
    for o, t, k in order:
        guarded(o, lambda o=o, t=t, k=k: tile_copy(o, t, k, place_at(o, t, k)).wait_send())


def spread_kernel(date_size, count, matchings, results, out, sem):
    d = lax.axis_index("date")
    copies = []
    for m in range(out.shape[0]):
        spot = m
        if count == date_size:
            spot = lax.rem(matchings[d, m] - d + date_size, date_size)
        for c in range(2):
            copies.append(
                pltpu.make_async_copy(
                    results.at[spot, pl.ds(c * PATCH, PATCH)], out.at[m, c, 0], sem.at[m, c]
                )
            )
    for copy in copies:
        copy.start()
    for copy in copies:
        copy.wait()


def per_device(az_size, date_size, image_stack, tap_weights, offsets, matchings):
    lines, samples = image_stack.shape[2:]
    assert image_stack.shape[1] == 1 and lines == PATCH
    matches = matchings.shape[0]
    count = min(matches, date_size)
    columns = samples // HALF + 1
    by_date = matchings.T
    hbm = pl.BlockSpec(memory_space=pltpu.HBM)
    vmem = pl.BlockSpec(memory_space=pltpu.VMEM)
    smem = pl.BlockSpec(memory_space=pltpu.SMEM)
    constants = tables()
    extra = [by_date] if count < date_size else []
    results = pl.pallas_call(
        functools.partial(stack_kernel, az_size, date_size, count),
        out_shape=pltpu.VMEM((count, 2 * lines, samples), jnp.float32),
        in_specs=[hbm] * 4 + [smem] * len(extra),
        out_specs=vmem,
        scratch_shapes=[
            pltpu.VMEM(image_stack.shape, jnp.float32),
            pltpu.VMEM(tap_weights.shape, jnp.float32),
            pltpu.VMEM(offsets.shape, jnp.int32),
            pltpu.VMEM(constants.shape, jnp.bfloat16),
            pltpu.VMEM((2, 2, RIM, samples), jnp.float32),
            pltpu.VMEM((2, lines, samples), jnp.bfloat16),
            pltpu.VMEM((HALF, 4 * HALF), jnp.bfloat16),
            pltpu.VMEM((date_size, 2, 4 * HALF, samples), jnp.bfloat16),
            pltpu.VMEM((date_size, 3, HALF, 4 * HALF), jnp.bfloat16),
            pltpu.VMEM((columns, 2 * PATCH, LANES), jnp.float32),
            pltpu.VMEM((columns * PATCH, LANES), jnp.bfloat16),
            pltpu.VMEM((columns, 2 * PATCH, LANES), jnp.bfloat16),
            pltpu.VMEM((samples, 2 * LANES), jnp.bfloat16),
            pltpu.SemaphoreType.DMA((4,)),
            pltpu.SemaphoreType.DMA((2,)),
            pltpu.SemaphoreType.DMA((2,)),
            pltpu.SemaphoreType.DMA((date_size, 3, 2)),
            pltpu.SemaphoreType.DMA((date_size, 3, 2)),
        ],
        compiler_params=pltpu.CompilerParams(
            collective_id=0, has_side_effects=True, vmem_limit_bytes=VMEM_LIMIT
        ),
    )(image_stack, tap_weights, offsets, jnp.asarray(constants), *extra)
    return pl.pallas_call(
        functools.partial(spread_kernel, date_size, count),
        out_shape=jax.ShapeDtypeStruct((matches, 2, 1, lines, samples), jnp.float32),
        in_specs=[smem, vmem],
        out_specs=hbm,
        scratch_shapes=[pltpu.SemaphoreType.DMA((matches, 2))],
        compiler_params=pltpu.CompilerParams(vmem_limit_bytes=VMEM_LIMIT),
    )(by_date, results)


def solution(mesh):
    placed = (
        P(None, ("parts", "date"), "az", "rg"),
        P(None, ("parts", "date"), "az"),
        P(("parts", "date"), "az"),
        P(),
    )
    assert mesh.shape["rg"] == 2
    return jax.shard_map(
        functools.partial(per_device, mesh.shape["az"], mesh.shape["date"]),
        mesh=mesh,
        in_specs=placed,
        out_specs=P(None, None, ("parts", "date"), "az", "rg"),
        check_vma=False,
    )
```

```python
import functools
import math

import jax
import jax.numpy as jnp
import ml_dtypes
import numpy as np
from jax import lax
from jax.experimental import pallas as pl
from jax.experimental.pallas import tpu as pltpu
from jax.sharding import PartitionSpec as P

TAPS = 8
SHIFT_MAX = 12
PATCH = 64
HALF = PATCH // 2
RIM = SHIFT_MAX + TAPS // 2
GROUPS = 4
LANES = GROUPS * PATCH
MESH = pl.DeviceIdType.MESH
BF16 = ml_dtypes.bfloat16
PLACE = {1: 0, 0: 1, -1: 2}


def fourier_table(sine_sign, table_scale):
    ids = np.arange(PATCH)
    angles = ((ids[:, None] * ids[None, :]) % PATCH) * (2.0 * math.pi / PATCH)
    cosine = np.cos(angles) * table_scale
    sine = np.sin(angles) * (sine_sign * table_scale)
    table = np.block([[cosine, -sine], [sine, cosine]]).astype(np.float32)
    return table.astype(BF16).astype(np.float32)


def tables():
    forward = fourier_table(1.0, 1.0)
    inverse = fourier_table(-1.0, 1.0 / PATCH)
    window = np.sin(math.pi * (np.arange(PATCH, dtype=np.float32) + 0.5) / PATCH) ** 2
    wide = 2 * PATCH
    line_in = np.zeros((2, wide, 2, GROUPS, PATCH), np.float32)
    line_out = np.zeros((2, PATCH, 2, GROUPS, PATCH), np.float32)
    split_f = forward.reshape(2, PATCH, 2, PATCH)
    split_i = inverse.reshape(2, PATCH, 2, PATCH)
    for r in range(3):
        line_in[:, r * HALF : r * HALF + PATCH, :, r] = split_f
        for line in range(PATCH):
            u = line + HALF - HALF * r
            if 0 <= u < PATCH:
                line_out[:, line, :, r] = split_i[:, :, :, u].transpose(2, 0, 1) * window[u]
    line_in = line_in.reshape(2 * wide, 2 * LANES).astype(BF16)
    line_out = line_out.reshape(wide, 2 * LANES)
    high = line_out.astype(BF16)
    low = (line_out - high.astype(np.float32)).astype(BF16)
    ids = np.arange(LANES)
    gap = (ids[:, None] - ids[None, :]) % PATCH
    same = ids[:, None] // PATCH == ids[None, :] // PATCH
    ring = (((gap <= 1) | (gap == PATCH - 1)) & same).astype(BF16)
    turns = np.concatenate([forward.T, inverse.T], axis=0).astype(BF16)
    rows = np.broadcast_to(np.tile(window, 2)[:, None], (wide, wide)).astype(np.float32)
    rows_high = rows.astype(BF16)
    rows_low = (rows - rows_high.astype(np.float32)).astype(BF16)
    last = np.concatenate([ring, turns, np.concatenate([rows_high, rows_low], axis=0)], axis=1)
    return np.concatenate([line_in, high, low, last], axis=0)


def stack_kernel(
    az_size, date_size, count, image_hbm, taps_hbm, offsets_hbm, table_hbm, *rest,
):
    if count < date_size:
        matchings, *rest = rest
    (
        out, image, taps, offsets, table, halo, tile, pack, wide, marg, spec, power_sum, shaped,
        back, load_sem, halo_send, halo_recv, send_sem, recv_sem,
    ) = rest
    a = lax.axis_index("az")
    d = lax.axis_index("date")
    g = lax.axis_index("rg")
    lines = image.shape[2]
    samples = image.shape[3]
    loads = [
        pltpu.make_async_copy(source, target, load_sem.at[i])
        for i, (source, target) in enumerate(
            ((offsets_hbm, offsets), (taps_hbm, taps), (image_hbm, image), (table_hbm, table))
        )
    ]
    has_up = a > 0
    has_down = a < az_size - 1
    exists = {-1: has_up, 0: None, 1: has_down}

    def guarded(step, body):
        if exists[step] is None:
            body()
        else:
            pl.when(exists[step])(body)

    def place_at(az_step, date_step, other):
        return {
            "az": a + az_step,
            "date": lax.rem(d + date_step, date_size),
            "rg": 1 - g if other else g,
        }

    peers = [
        (o, t, k) for o in (-1, 0, 1) for t in range(date_size) for k in (0, 1)
        if (o, t, k) != (0, 0, 0)
    ]
    barrier = pltpu.get_barrier_semaphore()
    for o, t, k in peers:
        guarded(o, lambda o=o, t=t, k=k: pl.semaphore_signal(
            barrier, inc=1, device_id=place_at(o, t, k), device_id_type=MESH))
    for load in loads:
        load.start()
    rows_near = 1 + has_up.astype(jnp.int32) + has_down.astype(jnp.int32)
    pl.semaphore_wait(barrier, rows_near * (2 * date_size) - 1)

    def halo_copy(step, target_step):
        first = lines - RIM if step == 1 else 0
        slot = 0 if step == 1 else 1
        return pltpu.make_async_remote_copy(
            src_ref=image_hbm.at[:, 0, pl.ds(first, RIM), :],
            dst_ref=halo.at[slot],
            send_sem=halo_send.at[slot],
            recv_sem=halo_recv.at[slot],
            device_id=place_at(target_step, 0, 0),
            device_id_type=MESH,
        )

    for step in (1, -1):
        guarded(step, lambda step=step: halo_copy(step, step).start())

    @pl.when(jnp.logical_not(has_up))
    def _():
        halo[0] = jnp.zeros(halo.shape[1:], halo.dtype)
        wide[:, :, 0:HALF] = jnp.zeros((date_size, 2, HALF, wide.shape[3]), wide.dtype)
        marg[:, 0] = jnp.zeros((date_size,) + marg.shape[2:], marg.dtype)

    @pl.when(jnp.logical_not(has_down))
    def _():
        halo[1] = jnp.zeros(halo.shape[1:], halo.dtype)
        wide[:, :, 3 * HALF :] = jnp.zeros((date_size, 2, HALF, wide.shape[3]), wide.dtype)
        marg[:, 2] = jnp.zeros((date_size,) + marg.shape[2:], marg.dtype)

    for load in loads[:3]:
        load.wait()
    span = lines + 2 * RIM
    source = lax.broadcasted_iota(jnp.int32, (span, lines), 0)
    place = lax.broadcasted_iota(jnp.int32, (span, lines), 1)
    gap = source - place - (RIM - (TAPS // 2 - 1)) - offsets[0:1, :]
    band = jnp.zeros((span, lines), jnp.float32)
    for k in range(TAPS):
        band = jnp.where(gap == k, taps[k], band)

    guarded(-1, lambda: halo_copy(1, -1).wait_recv())
    guarded(1, lambda: halo_copy(-1, 1).wait_recv())
    stacked = jnp.concatenate(
        [
            jnp.concatenate([halo[0, c], image[c, 0], halo[1, c]], axis=0)
            for c in range(2)
        ],
        axis=1,
    )
    both = lax.dot_general(
        band, stacked, (((0,), (0,)), ((), ())),
        precision=lax.Precision.HIGHEST, preferred_element_type=jnp.float32,
    )
    results = [both[:, :samples], both[:, samples:]]
    parts = []
    for c in range(2):
        wide[0, c, HALF : HALF + lines] = results[c].astype(jnp.bfloat16)
        tile[c] = results[c].astype(jnp.bfloat16)
        edge = jnp.where(g == 0, results[c][:, samples - HALF :], results[c][:, :HALF])
        parts += [edge[:HALF], edge[HALF:]]
    pack[...] = jnp.concatenate(parts, axis=1).astype(jnp.bfloat16)

    taken = {1: (HALF, HALF, 0), 0: (0, lines, HALF), -1: (0, HALF, HALF + lines)}

    def tile_copy(o, t, other, target):
        slot = (date_size - t) % date_size
        spot = PLACE[o]
        if other:
            src, dst = pack, marg.at[slot, spot]
        else:
            first, size, land = taken[o]
            src = tile.at[:, pl.ds(first, size), :]
            dst = wide.at[slot, :, pl.ds(land, size), :]
        return pltpu.make_async_remote_copy(
            src_ref=src, dst_ref=dst,
            send_sem=send_sem.at[t, spot, other],
            recv_sem=recv_sem.at[slot, spot, other],
            device_id=target, device_id_type=MESH,
        )

    order = sorted(peers, key=lambda p: (p[1], abs(p[0]), p[2]))
    for o, t, k in order:
        guarded(o, lambda o=o, t=t, k=k: tile_copy(o, t, k, place_at(o, t, k)).start())

    def arrived(slot):
        for o, t, k in order:
            if (date_size - t) % date_size == slot:
                guarded(-o, lambda o=o, t=t, k=k: tile_copy(
                    o, t, k, place_at(-o, slot, k)).wait_recv())

    def turned(slot):
        core = jnp.concatenate([wide[slot, 0], wide[slot, 1]], axis=0).astype(jnp.float32).T
        blocks = []
        for c in range(2):
            for spot, h in ((0, 1), (1, 0), (1, 1), (2, 0)):
                first = (2 * c + h) * HALF
                blocks.append(marg[slot, spot][:, first : first + HALF].astype(jnp.float32))
        side = jnp.concatenate(blocks, axis=0)
        side = jnp.concatenate([side, jnp.zeros((side.shape[0], 128 - HALF), jnp.float32)], axis=1)
        side = side.T[:HALF]
        zero = jnp.zeros_like(side)
        left = jnp.where(g == 0, zero, side)
        right = jnp.where(g == 0, side, zero)
        return jnp.concatenate([left, core, right], axis=0)

    def filtered(own, other):
        wide_lines = 2 * PATCH
        own_real, own_imag = own[:, :wide_lines], own[:, wide_lines:]
        other_real, other_imag = other[:, :wide_lines], other[:, wide_lines:]
        real_part = own_real * other_real + own_imag * other_imag
        imag_part = own_imag * other_real - own_real * other_imag
        ifg = jnp.concatenate([real_part, imag_part], axis=1).astype(jnp.bfloat16)
        spectra = jnp.dot(
            ifg, table[0 : 2 * wide_lines], preferred_element_type=jnp.float32
        ).astype(jnp.bfloat16)
        ring = table[4 * wide_lines :, 0:LANES]
        forward = table[4 * wide_lines : 5 * wide_lines, LANES : LANES + wide_lines]
        inverse = table[5 * wide_lines :, LANES : LANES + wide_lines]
        rows = [
            table[i * wide_lines : (i + 1) * wide_lines, LANES + wide_lines :].astype(jnp.float32)
            for i in (4, 5)
        ]
        weights = rows[0] + rows[1]
        weights = jnp.concatenate([weights] * (LANES // wide_lines), axis=1)
        columns = samples // HALF + 1
        for q in range(columns):
            rows = spectra[q * HALF : q * HALF + PATCH]
            block = jnp.concatenate([rows[:, :LANES], rows[:, LANES:]], axis=0)
            spectrum = jnp.dot(forward, block, preferred_element_type=jnp.float32)
            spec[q] = spectrum
            real, imag = spectrum[:PATCH], spectrum[PATCH:]
            power = real * real + imag * imag
            summed = power + pltpu.roll(power, 1, 0) + pltpu.roll(power, PATCH - 1, 0)
            power_sum[q * PATCH : (q + 1) * PATCH] = summed.astype(jnp.bfloat16)
        smooth = jnp.dot(power_sum[...], ring, preferred_element_type=jnp.float32)
        gains = lax.rsqrt(lax.rsqrt(1.0 + smooth * (1.0 / (9.0 * PATCH * PATCH))))
        for q in range(columns):
            gain = gains[q * PATCH : (q + 1) * PATCH]
            shaped[q, :PATCH] = (spec[q, :PATCH] * gain).astype(jnp.bfloat16)
            shaped[q, PATCH:] = (spec[q, PATCH:] * gain).astype(jnp.bfloat16)
        held = None
        for q in range(columns):
            ranged = jnp.dot(inverse, shaped[q], preferred_element_type=jnp.float32) * weights
            if held is not None:
                for c in range(2):
                    joined = held[c] + ranged[c * PATCH : c * PATCH + HALF]
                    back[(q - 1) * HALF : q * HALF, c * LANES : (c + 1) * LANES] = joined.astype(
                        jnp.bfloat16
                    )
            held = [ranged[c * PATCH + HALF : (c + 1) * PATCH] for c in range(2)]
        split = lax.dot_general(
            table[2 * wide_lines : 4 * wide_lines], back[...], (((1,), (1,)), ((), ())),
            preferred_element_type=jnp.float32,
        )
        return split[:wide_lines] + split[wide_lines:]

    loads[3].wait()
    arrived(0)
    own = turned(0)
    if count == date_size:
        for j in range(count):
            if j:
                arrived(j)
            out[j] = filtered(own, turned(j) if j else own)
    else:
        for j in range(1, date_size):
            arrived(j)
        for m in range(count):
            slot = lax.rem(matchings[d, m] - d + date_size, date_size)
            out[m] = filtered(own, turned(slot))

    for step in (1, -1):
        guarded(step, lambda step=step: halo_copy(step, step).wait_send())
    for o, t, k in order:
        guarded(o, lambda o=o, t=t, k=k: tile_copy(o, t, k, place_at(o, t, k)).wait_send())


def spread_kernel(date_size, count, matchings, results, out, sem):
    d = lax.axis_index("date")
    copies = []
    for m in range(out.shape[0]):
        spot = m
        if count == date_size:
            spot = lax.rem(matchings[d, m] - d + date_size, date_size)
        for c in range(2):
            copies.append(
                pltpu.make_async_copy(
                    results.at[spot, pl.ds(c * PATCH, PATCH)], out.at[m, c, 0], sem.at[m, c]
                )
            )
    for copy in copies:
        copy.start()
    for copy in copies:
        copy.wait()


def per_device(az_size, date_size, image_stack, tap_weights, offsets, matchings):
    lines, samples = image_stack.shape[2:]
    assert image_stack.shape[1] == 1 and lines == PATCH
    matches = matchings.shape[0]
    count = min(matches, date_size)
    columns = samples // HALF + 1
    by_date = matchings.T
    hbm = pl.BlockSpec(memory_space=pltpu.HBM)
    vmem = pl.BlockSpec(memory_space=pltpu.VMEM)
    smem = pl.BlockSpec(memory_space=pltpu.SMEM)
    constants = tables()
    extra = [by_date] if count < date_size else []
    results = pl.pallas_call(
        functools.partial(stack_kernel, az_size, date_size, count),
        out_shape=pltpu.VMEM((count, 2 * lines, samples), jnp.float32),
        in_specs=[hbm] * 4 + [smem] * len(extra),
        out_specs=vmem,
        scratch_shapes=[
            pltpu.VMEM(image_stack.shape, jnp.float32),
            pltpu.VMEM(tap_weights.shape, jnp.float32),
            pltpu.VMEM(offsets.shape, jnp.int32),
            pltpu.VMEM(constants.shape, jnp.bfloat16),
            pltpu.VMEM((2, 2, RIM, samples), jnp.float32),
            pltpu.VMEM((2, lines, samples), jnp.bfloat16),
            pltpu.VMEM((HALF, 4 * HALF), jnp.bfloat16),
            pltpu.VMEM((date_size, 2, 4 * HALF, samples), jnp.bfloat16),
            pltpu.VMEM((date_size, 3, HALF, 4 * HALF), jnp.bfloat16),
            pltpu.VMEM((columns, 2 * PATCH, LANES), jnp.float32),
            pltpu.VMEM((columns * PATCH, LANES), jnp.bfloat16),
            pltpu.VMEM((columns, 2 * PATCH, LANES), jnp.bfloat16),
            pltpu.VMEM((samples, 2 * LANES), jnp.bfloat16),
            pltpu.SemaphoreType.DMA((4,)),
            pltpu.SemaphoreType.DMA((2,)),
            pltpu.SemaphoreType.DMA((2,)),
            pltpu.SemaphoreType.DMA((date_size, 3, 2)),
            pltpu.SemaphoreType.DMA((date_size, 3, 2)),
        ],
        compiler_params=pltpu.CompilerParams(collective_id=0, has_side_effects=True),
    )(image_stack, tap_weights, offsets, jnp.asarray(constants), *extra)
    return pl.pallas_call(
        functools.partial(spread_kernel, date_size, count),
        out_shape=jax.ShapeDtypeStruct((matches, 2, 1, lines, samples), jnp.float32),
        in_specs=[smem, vmem],
        out_specs=hbm,
        scratch_shapes=[pltpu.SemaphoreType.DMA((matches, 2))],
        compiler_params=pltpu.CompilerParams(vmem_limit_bytes=16 << 20),
    )(by_date, results)


def solution(mesh):
    placed = (
        P(None, ("parts", "date"), "az", "rg"),
        P(None, ("parts", "date"), "az"),
        P(("parts", "date"), "az"),
        P(),
    )
    assert mesh.shape["rg"] == 2
    return jax.shard_map(
        functools.partial(per_device, mesh.shape["az"], mesh.shape["date"]),
        mesh=mesh,
        in_specs=placed,
        out_specs=P(None, None, ("parts", "date"), "az", "rg"),
        check_vma=False,
    )
```

```python
import functools
import math

import jax
import jax.numpy as jnp
import ml_dtypes
import numpy as np
from jax import lax
from jax.experimental import pallas as pl
from jax.experimental.pallas import tpu as pltpu
from jax.sharding import PartitionSpec as P

TAPS = 8
SHIFT_MAX = 12
PATCH = 64
HALF = PATCH // 2
RIM = SHIFT_MAX + TAPS // 2
REACH = RIM + HALF
GROUPS = 4
LANES = GROUPS * PATCH
MESH = pl.DeviceIdType.MESH
BF16 = ml_dtypes.bfloat16
PLACE = {1: 0, 0: 1, -1: 2}


def fourier_table(sine_sign, table_scale):
    ids = np.arange(PATCH)
    angles = ((ids[:, None] * ids[None, :]) % PATCH) * (2.0 * math.pi / PATCH)
    cosine = np.cos(angles) * table_scale
    sine = np.sin(angles) * (sine_sign * table_scale)
    table = np.block([[cosine, -sine], [sine, cosine]]).astype(np.float32)
    return table.astype(BF16).astype(np.float32)


def tables():
    forward = fourier_table(1.0, 1.0)
    inverse = fourier_table(-1.0, 1.0 / PATCH)
    window = np.sin(math.pi * (np.arange(PATCH, dtype=np.float32) + 0.5) / PATCH) ** 2
    wide = 2 * PATCH
    line_in = np.zeros((2, wide, 2, GROUPS, PATCH), np.float32)
    line_out = np.zeros((2, PATCH, 2, GROUPS, PATCH), np.float32)
    split_f = forward.reshape(2, PATCH, 2, PATCH)
    split_i = inverse.reshape(2, PATCH, 2, PATCH)
    for r in range(3):
        line_in[:, r * HALF : r * HALF + PATCH, :, r] = split_f
        for line in range(PATCH):
            u = line + HALF - HALF * r
            if 0 <= u < PATCH:
                line_out[:, line, :, r] = split_i[:, :, :, u].transpose(2, 0, 1) * window[u]
    line_in = line_in.reshape(2 * wide, 2 * LANES).astype(BF16)
    line_out = line_out.reshape(wide, 2 * LANES)
    high = line_out.astype(BF16)
    low = (line_out - high.astype(np.float32)).astype(BF16)
    ids = np.arange(LANES)
    gap = (ids[:, None] - ids[None, :]) % PATCH
    same = ids[:, None] // PATCH == ids[None, :] // PATCH
    ring = (((gap <= 1) | (gap == PATCH - 1)) & same).astype(BF16)
    turns = np.concatenate([forward.T, inverse.T], axis=0).astype(BF16)
    rows = np.broadcast_to(np.tile(window, 2)[:, None], (wide, wide)).astype(np.float32)
    rows_high = rows.astype(BF16)
    rows_low = (rows - rows_high.astype(np.float32)).astype(BF16)
    last = np.concatenate([ring, turns, np.concatenate([rows_high, rows_low], axis=0)], axis=1)
    return np.concatenate([line_in, high, low, last], axis=0)


def stack_kernel(
    az_size, date_size, count, image_hbm, taps_hbm, offsets_hbm, table_hbm, *rest,
):
    if count < date_size:
        matchings, *rest = rest
    (
        out, image, taps, offsets, table, tile, pack, kernels, near, far, near_side, far_side,
        all_kernels, turned, spec, power_sum, shaped, back, load_sem, send_sem, recv_sem,
    ) = rest
    a = lax.axis_index("az")
    d = lax.axis_index("date")
    g = lax.axis_index("rg")
    lines = image.shape[2]
    samples = image.shape[3]
    loads = [
        pltpu.make_async_copy(source, target, load_sem.at[i])
        for i, (source, target) in enumerate(
            ((offsets_hbm, offsets), (taps_hbm, taps), (image_hbm, image), (table_hbm, table))
        )
    ]
    has_up = a > 0
    has_down = a < az_size - 1
    exists = {-1: has_up, 0: None, 1: has_down}

    def guarded(step, body):
        if exists[step] is None:
            body()
        else:
            pl.when(exists[step])(body)

    def place_at(az_step, date_step, other):
        return {
            "az": a + az_step,
            "date": lax.rem(d + date_step, date_size),
            "rg": 1 - g if other else g,
        }

    peers = [
        (o, t, k) for o in (-1, 0, 1) for t in range(date_size) for k in (0, 1)
        if (o, t, k) != (0, 0, 0)
    ]
    barrier = pltpu.get_barrier_semaphore()
    for o, t, k in peers:
        guarded(o, lambda o=o, t=t, k=k: pl.semaphore_signal(
            barrier, inc=1, device_id=place_at(o, t, k), device_id_type=MESH))
    for load in loads:
        load.start()
    @pl.when(jnp.logical_not(has_up))
    def _():
        near[:, :, 0:REACH] = jnp.zeros((2, 2, REACH, samples), near.dtype)
        far[:, :, 0:REACH] = jnp.zeros((date_size - 1, 2, REACH, samples), far.dtype)
        near_side[0] = jnp.zeros(near_side.shape[1:], near_side.dtype)
        far_side[:, 0] = jnp.zeros((date_size - 1,) + far_side.shape[2:], far_side.dtype)
        all_kernels[:, 0] = jnp.zeros((date_size,) + all_kernels.shape[2:], jnp.float32)

    @pl.when(jnp.logical_not(has_down))
    def _():
        near[:, :, REACH + lines :] = jnp.zeros((2, 2, REACH, samples), near.dtype)
        far[:, :, REACH + lines :] = jnp.zeros((date_size - 1, 2, REACH, samples), far.dtype)
        near_side[2] = jnp.zeros(near_side.shape[1:], near_side.dtype)
        far_side[:, 2] = jnp.zeros((date_size - 1,) + far_side.shape[2:], far_side.dtype)
        all_kernels[:, 2] = jnp.zeros((date_size,) + all_kernels.shape[2:], jnp.float32)

    for load in loads[:3]:
        load.wait()
    shifts = jnp.broadcast_to(offsets[0:1, :].astype(jnp.float32), (TAPS, lines))
    held = jnp.concatenate([taps[:, 0], shifts], axis=1)
    kernels[...] = held
    all_kernels[0, 1] = held
    parts = ([], [])
    for c in range(2):
        value = image[c, 0]
        high = value.astype(jnp.bfloat16)
        low = (value - high.astype(jnp.float32)).astype(jnp.bfloat16)
        for i, piece in enumerate((high, low)):
            tile[i, c] = piece
            near[i, c, REACH : REACH + lines] = piece
            piece = piece.astype(jnp.float32)
            edge = jnp.where(g == 0, piece[:, samples - HALF :], piece[:, :HALF])
            parts[i].extend([edge[:HALF], edge[HALF:]])
    for i in range(2):
        pack[i] = jnp.concatenate(parts[i], axis=1).astype(jnp.bfloat16)

    rows_near = 1 + has_up.astype(jnp.int32) + has_down.astype(jnp.int32)
    pl.semaphore_wait(barrier, rows_near * (2 * date_size) - 1)

    taken = {
        1: (lines - REACH, REACH, 0), 0: (0, lines, REACH), -1: (0, REACH, REACH + lines),
    }

    def send(o, t, kind, target):
        slot = (date_size - t) % date_size
        spot = PLACE[o]
        first, size, land = taken[o]
        if kind == 0 and t == 0:
            src = tile.at[:, :, pl.ds(first, size), :]
            dst = near.at[:, :, pl.ds(land, size), :]
        elif kind == 0:
            src = tile.at[0, :, pl.ds(first, size), :]
            dst = far.at[slot - 1, :, pl.ds(land, size), :]
        elif kind == 1 and t == 0:
            src, dst = pack, near_side.at[spot]
        elif kind == 1:
            src, dst = pack.at[0], far_side.at[slot - 1, spot]
        else:
            src, dst = kernels, all_kernels.at[slot, spot]
        return pltpu.make_async_remote_copy(
            src_ref=src, dst_ref=dst,
            send_sem=send_sem.at[t, spot, kind],
            recv_sem=recv_sem.at[slot, spot, kind],
            device_id=target, device_id_type=MESH,
        )

    order = []
    for o, t, k in sorted(peers, key=lambda p: (p[1], p[1] == 0 or abs(p[0]), p[2])):
        order += [(o, t, 1, 1)] if k else [(o, t, 2, 0), (o, t, 0, 0)]
    for o, t, kind, k in order:
        guarded(o, lambda o=o, t=t, kind=kind, k=k: send(o, t, kind, place_at(o, t, k)).start())

    def arrived(slot):
        for o, t, kind, k in order:
            if (date_size - t) % date_size == slot:
                guarded(-o, lambda o=o, t=t, kind=kind, k=k: send(
                    o, t, kind, place_at(-o, slot, k)).wait_recv())

    span = lines + 2 * REACH
    wide_lines = 4 * HALF
    source = lax.broadcasted_iota(jnp.int32, (span, wide_lines), 0)
    place = lax.broadcasted_iota(jnp.int32, (span, wide_lines), 1)
    distance = (source - place - (RIM - (TAPS // 2 - 1))).astype(jnp.float32)

    def resample(slot):
        above, own_rows, below = (all_kernels[slot, i] for i in range(3))
        weights = jnp.concatenate(
            [above[:, HALF:lines], own_rows[:, :lines], below[:, :HALF]], axis=1
        )
        shift = jnp.concatenate(
            [above[:, lines + HALF :], own_rows[:, lines:], below[:, lines : lines + HALF]], axis=1
        )
        gap = distance - shift[0:1]
        band = jnp.zeros((span, wide_lines), jnp.float32)
        for k in range(TAPS):
            band = jnp.where(gap == float(k), weights[k : k + 1], band)
        band_high = band.astype(jnp.bfloat16)
        band_low = (band - band_high.astype(jnp.float32)).astype(jnp.bfloat16)
        band_both = jnp.concatenate([band_high, band_low], axis=1)
        total = None
        for i in range(1 if slot else 2):
            columns = []
            for c in range(2):
                columns.append(far[slot - 1, c] if slot else near[i, c])
            blank = []
            for c in range(2):
                rows = []
                for spot in range(3):
                    value = far_side[slot - 1, spot] if slot else near_side[spot, i]
                    value = value.astype(jnp.float32)
                    first = 2 * c * HALF
                    both = jnp.concatenate(
                        [value[:, first : first + HALF], value[:, first + HALF : first + 2 * HALF]],
                        axis=0,
                    )
                    rows.append(
                        (both[lines - REACH :], both, both[:REACH])[spot]
                    )
                blank.append(jnp.concatenate(rows, axis=0))
            blank.append(jnp.zeros((span, 128 - 2 * HALF), jnp.float32))
            columns.append(jnp.concatenate(blank, axis=1).astype(jnp.bfloat16))
            product = lax.dot_general(
                jnp.concatenate(columns, axis=1), band_both, (((0,), (0,)), ((), ())),
                preferred_element_type=jnp.float32,
            )
            product = product[:, :wide_lines] + product[:, wide_lines:]
            total = product if total is None else total + product
        total = total.astype(jnp.bfloat16).astype(jnp.float32)
        core = jnp.concatenate([total[:samples], total[samples : 2 * samples]], axis=1)
        side = total[2 * samples : 2 * samples + 2 * HALF]
        side = jnp.concatenate([side[:HALF], side[HALF:]], axis=1)
        zero = jnp.zeros_like(side)
        turned[slot, 0:HALF] = jnp.where(g == 0, zero, side)
        turned[slot, HALF : HALF + samples] = core
        turned[slot, HALF + samples :] = jnp.where(g == 0, side, zero)

    def filtered(own, other):
        wide_lines = 2 * PATCH
        own_real, own_imag = own[:, :wide_lines], own[:, wide_lines:]
        other_real, other_imag = other[:, :wide_lines], other[:, wide_lines:]
        real_part = own_real * other_real + own_imag * other_imag
        imag_part = own_imag * other_real - own_real * other_imag
        ifg = jnp.concatenate([real_part, imag_part], axis=1).astype(jnp.bfloat16)
        spectra = jnp.dot(
            ifg, table[0 : 2 * wide_lines], preferred_element_type=jnp.float32
        ).astype(jnp.bfloat16)
        ring = table[4 * wide_lines :, 0:LANES]
        forward = table[4 * wide_lines : 5 * wide_lines, LANES : LANES + wide_lines]
        inverse = table[5 * wide_lines :, LANES : LANES + wide_lines]
        rows = [
            table[i * wide_lines : (i + 1) * wide_lines, LANES + wide_lines :].astype(jnp.float32)
            for i in (4, 5)
        ]
        weights = rows[0] + rows[1]
        weights = jnp.concatenate([weights] * (LANES // wide_lines), axis=1)
        columns = samples // HALF + 1
        for q in range(columns):
            rows = spectra[q * HALF : q * HALF + PATCH]
            block = jnp.concatenate([rows[:, :LANES], rows[:, LANES:]], axis=0)
            spectrum = jnp.dot(forward, block, preferred_element_type=jnp.float32)
            spec[q] = spectrum
            real, imag = spectrum[:PATCH], spectrum[PATCH:]
            power = real * real + imag * imag
            summed = power + pltpu.roll(power, 1, 0) + pltpu.roll(power, PATCH - 1, 0)
            power_sum[q * PATCH : (q + 1) * PATCH] = summed.astype(jnp.bfloat16)
        smooth = jnp.dot(power_sum[...], ring, preferred_element_type=jnp.float32)
        gains = lax.rsqrt(lax.rsqrt(1.0 + smooth * (1.0 / (9.0 * PATCH * PATCH))))
        for q in range(columns):
            gain = gains[q * PATCH : (q + 1) * PATCH]
            shaped[q, :PATCH] = (spec[q, :PATCH] * gain).astype(jnp.bfloat16)
            shaped[q, PATCH:] = (spec[q, PATCH:] * gain).astype(jnp.bfloat16)
        held = None
        for q in range(columns):
            ranged = jnp.dot(inverse, shaped[q], preferred_element_type=jnp.float32) * weights
            if held is not None:
                for c in range(2):
                    joined = held[c] + ranged[c * PATCH : c * PATCH + HALF]
                    back[(q - 1) * HALF : q * HALF, c * LANES : (c + 1) * LANES] = joined.astype(
                        jnp.bfloat16
                    )
            held = [ranged[c * PATCH + HALF : (c + 1) * PATCH] for c in range(2)]
        split = lax.dot_general(
            table[2 * wide_lines : 4 * wide_lines], back[...], (((1,), (1,)), ((), ())),
            preferred_element_type=jnp.float32,
        )
        return split[:wide_lines] + split[wide_lines:]

    arrived(0)
    resample(0)
    loads[3].wait()
    if count == date_size:
        for j in range(count):
            if j:
                arrived(j)
                resample(j)
            out[j] = filtered(turned[0], turned[j])
    else:
        for j in range(1, date_size):
            arrived(j)
            resample(j)
        for m in range(count):
            slot = lax.rem(matchings[d, m] - d + date_size, date_size)
            out[m] = filtered(turned[0], turned[slot])

    for o, t, kind, k in order:
        guarded(o, lambda o=o, t=t, kind=kind, k=k: send(
            o, t, kind, place_at(o, t, k)).wait_send())


def spread_kernel(date_size, count, matchings, results, out, sem):
    d = lax.axis_index("date")
    copies = []
    for m in range(out.shape[0]):
        spot = m
        if count == date_size:
            spot = lax.rem(matchings[d, m] - d + date_size, date_size)
        for c in range(2):
            copies.append(
                pltpu.make_async_copy(
                    results.at[spot, pl.ds(c * PATCH, PATCH)], out.at[m, c, 0], sem.at[m, c]
                )
            )
    for copy in copies:
        copy.start()
    for copy in copies:
        copy.wait()


def per_device(az_size, date_size, image_stack, tap_weights, offsets, matchings):
    lines, samples = image_stack.shape[2:]
    assert image_stack.shape[1] == 1 and lines == PATCH
    matches = matchings.shape[0]
    count = min(matches, date_size)
    columns = samples // HALF + 1
    by_date = matchings.T
    hbm = pl.BlockSpec(memory_space=pltpu.HBM)
    vmem = pl.BlockSpec(memory_space=pltpu.VMEM)
    smem = pl.BlockSpec(memory_space=pltpu.SMEM)
    constants = tables()
    extra = [by_date] if count < date_size else []
    results = pl.pallas_call(
        functools.partial(stack_kernel, az_size, date_size, count),
        out_shape=pltpu.VMEM((count, 2 * lines, samples), jnp.float32),
        in_specs=[hbm] * 4 + [smem] * len(extra),
        out_specs=vmem,
        scratch_shapes=[
            pltpu.VMEM(image_stack.shape, jnp.float32),
            pltpu.VMEM(tap_weights.shape, jnp.float32),
            pltpu.VMEM(offsets.shape, jnp.int32),
            pltpu.VMEM(constants.shape, jnp.bfloat16),
            pltpu.VMEM((2, 2, lines, samples), jnp.bfloat16),
            pltpu.VMEM((2, HALF, 4 * HALF), jnp.bfloat16),
            pltpu.VMEM((TAPS, 2 * lines), jnp.float32),
            pltpu.VMEM((2, 2, lines + 2 * REACH, samples), jnp.bfloat16),
            pltpu.VMEM((date_size - 1, 2, lines + 2 * REACH, samples), jnp.bfloat16),
            pltpu.VMEM((3, 2, HALF, 4 * HALF), jnp.bfloat16),
            pltpu.VMEM((date_size - 1, 3, HALF, 4 * HALF), jnp.bfloat16),
            pltpu.VMEM((date_size, 3, TAPS, 2 * lines), jnp.float32),
            pltpu.VMEM((date_size, samples + 2 * HALF, 8 * HALF), jnp.float32),
            pltpu.VMEM((columns, 2 * PATCH, LANES), jnp.float32),
            pltpu.VMEM((columns * PATCH, LANES), jnp.bfloat16),
            pltpu.VMEM((columns, 2 * PATCH, LANES), jnp.bfloat16),
            pltpu.VMEM((samples, 2 * LANES), jnp.bfloat16),
            pltpu.SemaphoreType.DMA((4,)),
            pltpu.SemaphoreType.DMA((date_size, 3, 3)),
            pltpu.SemaphoreType.DMA((date_size, 3, 3)),
        ],
        compiler_params=pltpu.CompilerParams(collective_id=0, has_side_effects=True),
    )(image_stack, tap_weights, offsets, jnp.asarray(constants), *extra)
    return pl.pallas_call(
        functools.partial(spread_kernel, date_size, count),
        out_shape=jax.ShapeDtypeStruct((matches, 2, 1, lines, samples), jnp.float32),
        in_specs=[smem, vmem],
        out_specs=hbm,
        scratch_shapes=[pltpu.SemaphoreType.DMA((matches, 2))],
        compiler_params=pltpu.CompilerParams(vmem_limit_bytes=16 << 20),
    )(by_date, results)


def solution(mesh):
    placed = (
        P(None, ("parts", "date"), "az", "rg"),
        P(None, ("parts", "date"), "az"),
        P(("parts", "date"), "az"),
        P(),
    )
    assert mesh.shape["rg"] == 2
    return jax.shard_map(
        functools.partial(per_device, mesh.shape["az"], mesh.shape["date"]),
        mesh=mesh,
        in_specs=placed,
        out_specs=P(None, None, ("parts", "date"), "az", "rg"),
        check_vma=False,
    )
```

```python
import functools
import math

import jax
import jax.numpy as jnp
import ml_dtypes
import numpy as np
from jax import lax
from jax.experimental import pallas as pl
from jax.experimental.pallas import tpu as pltpu
from jax.sharding import PartitionSpec as P

TAPS = 8
SHIFT_MAX = 12
PATCH = 64
HALF = PATCH // 2
RIM = SHIFT_MAX + TAPS // 2
REACH = RIM + HALF
GROUPS = 4
LANES = GROUPS * PATCH
MESH = pl.DeviceIdType.MESH
BF16 = ml_dtypes.bfloat16
PLACE = {1: 0, 0: 1, -1: 2}


def fourier_table(sine_sign, table_scale):
    ids = np.arange(PATCH)
    angles = ((ids[:, None] * ids[None, :]) % PATCH) * (2.0 * math.pi / PATCH)
    cosine = np.cos(angles) * table_scale
    sine = np.sin(angles) * (sine_sign * table_scale)
    table = np.block([[cosine, -sine], [sine, cosine]]).astype(np.float32)
    return table.astype(BF16).astype(np.float32)


def tables():
    forward = fourier_table(1.0, 1.0)
    inverse = fourier_table(-1.0, 1.0 / PATCH)
    window = np.sin(math.pi * (np.arange(PATCH, dtype=np.float32) + 0.5) / PATCH) ** 2
    wide = 2 * PATCH
    line_in = np.zeros((2, wide, 2, GROUPS, PATCH), np.float32)
    line_out = np.zeros((2, PATCH, 2, GROUPS, PATCH), np.float32)
    split_f = forward.reshape(2, PATCH, 2, PATCH)
    split_i = inverse.reshape(2, PATCH, 2, PATCH)
    for r in range(3):
        line_in[:, r * HALF : r * HALF + PATCH, :, r] = split_f
        for line in range(PATCH):
            u = line + HALF - HALF * r
            if 0 <= u < PATCH:
                line_out[:, line, :, r] = split_i[:, :, :, u].transpose(2, 0, 1) * window[u]
    line_in = line_in.reshape(2 * wide, 2 * LANES).astype(BF16)
    line_out = line_out.reshape(wide, 2 * LANES)
    high = line_out.astype(BF16)
    low = (line_out - high.astype(np.float32)).astype(BF16)
    ids = np.arange(LANES)
    gap = (ids[:, None] - ids[None, :]) % PATCH
    same = ids[:, None] // PATCH == ids[None, :] // PATCH
    ring = (((gap <= 1) | (gap == PATCH - 1)) & same).astype(BF16)
    turns = np.concatenate([forward.T, inverse.T], axis=0).astype(BF16)
    rows = np.broadcast_to(np.tile(window, 2)[:, None], (wide, wide)).astype(np.float32)
    rows_high = rows.astype(BF16)
    rows_low = (rows - rows_high.astype(np.float32)).astype(BF16)
    last = np.concatenate([ring, turns, np.concatenate([rows_high, rows_low], axis=0)], axis=1)
    return np.concatenate([line_in, high, low, last], axis=0)


def stack_kernel(
    az_size, date_size, count, image_hbm, taps_hbm, offsets_hbm, table_hbm, *rest,
):
    if count < date_size:
        matchings, *rest = rest
    (
        out, image, taps, offsets, table, tile, pack, kernels, near, near_side,
        all_kernels, turned, spec, power_sum, shaped, back, load_sem, send_sem, recv_sem,
    ) = rest
    a = lax.axis_index("az")
    d = lax.axis_index("date")
    g = lax.axis_index("rg")
    lines = image.shape[2]
    samples = image.shape[3]
    loads = [
        pltpu.make_async_copy(source, target, load_sem.at[i])
        for i, (source, target) in enumerate(
            ((offsets_hbm, offsets), (taps_hbm, taps), (image_hbm, image), (table_hbm, table))
        )
    ]
    has_up = a > 0
    has_down = a < az_size - 1
    exists = {-1: has_up, 0: None, 1: has_down}

    def guarded(step, body):
        if exists[step] is None:
            body()
        else:
            pl.when(exists[step])(body)

    def place_at(az_step, date_step, other):
        return {
            "az": a + az_step,
            "date": lax.rem(d + date_step, date_size),
            "rg": 1 - g if other else g,
        }

    peers = [
        (o, 0, k) for o in (-1, 0, 1) for k in (0, 1) if (o, k) != (0, 0)
    ] + [(0, t, 0) for t in range(1, date_size)]
    barrier = pltpu.get_barrier_semaphore()
    for o, t, k in peers:
        guarded(o, lambda o=o, t=t, k=k: pl.semaphore_signal(
            barrier, inc=1, device_id=place_at(o, t, k), device_id_type=MESH))
    for load in loads:
        load.start()
    @pl.when(jnp.logical_not(has_up))
    def _():
        near[:, :, 0:REACH] = jnp.zeros((2, 2, REACH, samples), near.dtype)
        near_side[0] = jnp.zeros(near_side.shape[1:], near_side.dtype)
        all_kernels[0] = jnp.zeros(all_kernels.shape[1:], jnp.float32)

    @pl.when(jnp.logical_not(has_down))
    def _():
        near[:, :, REACH + lines :] = jnp.zeros((2, 2, REACH, samples), near.dtype)
        near_side[2] = jnp.zeros(near_side.shape[1:], near_side.dtype)
        all_kernels[2] = jnp.zeros(all_kernels.shape[1:], jnp.float32)

    for load in loads[:3]:
        load.wait()
    shifts = jnp.broadcast_to(offsets[0:1, :].astype(jnp.float32), (TAPS, lines))
    held = jnp.concatenate([taps[:, 0], shifts], axis=1)
    kernels[...] = held
    all_kernels[1] = held
    parts = ([], [])
    for c in range(2):
        value = image[c, 0]
        high = value.astype(jnp.bfloat16)
        low = (value - high.astype(jnp.float32)).astype(jnp.bfloat16)
        for i, piece in enumerate((high, low)):
            tile[i, c] = piece
            near[i, c, REACH : REACH + lines] = piece
            piece = piece.astype(jnp.float32)
            edge = jnp.where(g == 0, piece[:, samples - HALF :], piece[:, :HALF])
            parts[i].extend([edge[:HALF], edge[HALF:]])
    for i in range(2):
        pack[i] = jnp.concatenate(parts[i], axis=1).astype(jnp.bfloat16)

    rows_near = 1 + has_up.astype(jnp.int32) + has_down.astype(jnp.int32)
    pl.semaphore_wait(barrier, rows_near * 2 + date_size - 2)

    taken = {
        1: (lines - REACH, REACH, 0), 0: (0, lines, REACH), -1: (0, REACH, REACH + lines),
    }

    def send(o, t, kind, target):
        slot = (date_size - t) % date_size
        spot = PLACE[o]
        first, size, land = taken[o]
        if t:
            src, dst = turned.at[0], turned.at[slot]
        elif kind == 0:
            src = tile.at[:, :, pl.ds(first, size), :]
            dst = near.at[:, :, pl.ds(land, size), :]
        elif kind == 1:
            src, dst = pack, near_side.at[spot]
        else:
            src, dst = kernels, all_kernels.at[spot]
        return pltpu.make_async_remote_copy(
            src_ref=src, dst_ref=dst,
            send_sem=send_sem.at[t, spot, kind],
            recv_sem=recv_sem.at[slot, spot, kind],
            device_id=target, device_id_type=MESH,
        )

    order = []
    for o, t, k in sorted(peers, key=lambda p: (p[1], p[2])):
        if t:
            order += [(o, t, 0, 0)]
        else:
            order += [(o, t, 1, 1)] if k else [(o, t, 2, 0), (o, t, 0, 0)]

    def begin(o, t, kind, k):
        guarded(o, lambda: send(o, t, kind, place_at(o, t, k)).start())

    for item in order:
        if item[1] == 0:
            begin(*item)

    def arrived(slot):
        for o, t, kind, k in order:
            if (date_size - t) % date_size == slot:
                guarded(-o, lambda o=o, t=t, kind=kind, k=k: send(
                    o, t, kind, place_at(-o, slot, k)).wait_recv())

    span = lines + 2 * REACH
    wide_lines = 4 * HALF
    source = lax.broadcasted_iota(jnp.int32, (span, wide_lines), 0)
    place = lax.broadcasted_iota(jnp.int32, (span, wide_lines), 1)
    distance = (source - place - (RIM - (TAPS // 2 - 1))).astype(jnp.float32)

    def resample():
        above, own_rows, below = (all_kernels[i] for i in range(3))
        weights = jnp.concatenate(
            [above[:, HALF:lines], own_rows[:, :lines], below[:, :HALF]], axis=1
        )
        shift = jnp.concatenate(
            [above[:, lines + HALF :], own_rows[:, lines:], below[:, lines : lines + HALF]], axis=1
        )
        gap = distance - shift[0:1]
        band = jnp.zeros((span, wide_lines), jnp.float32)
        for k in range(TAPS):
            band = jnp.where(gap == float(k), weights[k : k + 1], band)
        band_high = band.astype(jnp.bfloat16)
        band_low = (band - band_high.astype(jnp.float32)).astype(jnp.bfloat16)
        band_both = jnp.concatenate([band_high, band_low], axis=1)
        total = None
        for i in range(2):
            columns = []
            for c in range(2):
                columns.append(near[i, c])
            blank = []
            for c in range(2):
                rows = []
                for spot in range(3):
                    value = near_side[spot, i].astype(jnp.float32)
                    first = 2 * c * HALF
                    both = jnp.concatenate(
                        [value[:, first : first + HALF], value[:, first + HALF : first + 2 * HALF]],
                        axis=0,
                    )
                    rows.append(
                        (both[lines - REACH :], both, both[:REACH])[spot]
                    )
                blank.append(jnp.concatenate(rows, axis=0))
            blank.append(jnp.zeros((span, 128 - 2 * HALF), jnp.float32))
            columns.append(jnp.concatenate(blank, axis=1).astype(jnp.bfloat16))
            product = lax.dot_general(
                jnp.concatenate(columns, axis=1), band_both, (((0,), (0,)), ((), ())),
                preferred_element_type=jnp.float32,
            )
            product = product[:, :wide_lines] + product[:, wide_lines:]
            total = product if total is None else total + product
        core = jnp.concatenate([total[:samples], total[samples : 2 * samples]], axis=1)
        side = total[2 * samples : 2 * samples + 2 * HALF]
        side = jnp.concatenate([side[:HALF], side[HALF:]], axis=1)
        zero = jnp.zeros_like(side)
        turned[0, 0:HALF] = jnp.where(g == 0, zero, side).astype(jnp.bfloat16)
        turned[0, HALF : HALF + samples] = core.astype(jnp.bfloat16)
        turned[0, HALF + samples :] = jnp.where(g == 0, side, zero).astype(jnp.bfloat16)

    def filtered(own, other):
        wide_lines = 2 * PATCH
        own, other = own.astype(jnp.float32), other.astype(jnp.float32)
        own_real, own_imag = own[:, :wide_lines], own[:, wide_lines:]
        other_real, other_imag = other[:, :wide_lines], other[:, wide_lines:]
        real_part = own_real * other_real + own_imag * other_imag
        imag_part = own_imag * other_real - own_real * other_imag
        ifg = jnp.concatenate([real_part, imag_part], axis=1).astype(jnp.bfloat16)
        spectra = jnp.dot(
            ifg, table[0 : 2 * wide_lines], preferred_element_type=jnp.float32
        ).astype(jnp.bfloat16)
        ring = table[4 * wide_lines :, 0:LANES]
        forward = table[4 * wide_lines : 5 * wide_lines, LANES : LANES + wide_lines]
        inverse = table[5 * wide_lines :, LANES : LANES + wide_lines]
        rows = [
            table[i * wide_lines : (i + 1) * wide_lines, LANES + wide_lines :].astype(jnp.float32)
            for i in (4, 5)
        ]
        weights = rows[0] + rows[1]
        weights = jnp.concatenate([weights] * (LANES // wide_lines), axis=1)
        columns = samples // HALF + 1
        for q in range(columns):
            rows = spectra[q * HALF : q * HALF + PATCH]
            block = jnp.concatenate([rows[:, :LANES], rows[:, LANES:]], axis=0)
            spectrum = jnp.dot(forward, block, preferred_element_type=jnp.float32)
            spec[q] = spectrum
            real, imag = spectrum[:PATCH], spectrum[PATCH:]
            power = real * real + imag * imag
            summed = power + pltpu.roll(power, 1, 0) + pltpu.roll(power, PATCH - 1, 0)
            power_sum[q * PATCH : (q + 1) * PATCH] = summed.astype(jnp.bfloat16)
        smooth = jnp.dot(power_sum[...], ring, preferred_element_type=jnp.float32)
        gains = lax.rsqrt(lax.rsqrt(1.0 + smooth * (1.0 / (9.0 * PATCH * PATCH))))
        for q in range(columns):
            gain = gains[q * PATCH : (q + 1) * PATCH]
            shaped[q, :PATCH] = (spec[q, :PATCH] * gain).astype(jnp.bfloat16)
            shaped[q, PATCH:] = (spec[q, PATCH:] * gain).astype(jnp.bfloat16)
        held = None
        for q in range(columns):
            ranged = jnp.dot(inverse, shaped[q], preferred_element_type=jnp.float32) * weights
            if held is not None:
                for c in range(2):
                    joined = held[c] + ranged[c * PATCH : c * PATCH + HALF]
                    back[(q - 1) * HALF : q * HALF, c * LANES : (c + 1) * LANES] = joined.astype(
                        jnp.bfloat16
                    )
            held = [ranged[c * PATCH + HALF : (c + 1) * PATCH] for c in range(2)]
        split = lax.dot_general(
            table[2 * wide_lines : 4 * wide_lines], back[...], (((1,), (1,)), ((), ())),
            preferred_element_type=jnp.float32,
        )
        return split[:wide_lines] + split[wide_lines:]

    arrived(0)
    resample()
    for item in order:
        if item[1]:
            begin(*item)
    loads[3].wait()
    if count == date_size:
        for j in range(count):
            if j:
                arrived(j)
            out[j] = filtered(turned[0], turned[j])
    else:
        for j in range(1, date_size):
            arrived(j)
        for m in range(count):
            slot = lax.rem(matchings[d, m] - d + date_size, date_size)
            out[m] = filtered(turned[0], turned[slot])

    for o, t, kind, k in order:
        guarded(o, lambda o=o, t=t, kind=kind, k=k: send(
            o, t, kind, place_at(o, t, k)).wait_send())


def spread_kernel(date_size, count, matchings, results, out, sem):
    d = lax.axis_index("date")
    copies = []
    for m in range(out.shape[0]):
        spot = m
        if count == date_size:
            spot = lax.rem(matchings[d, m] - d + date_size, date_size)
        for c in range(2):
            copies.append(
                pltpu.make_async_copy(
                    results.at[spot, pl.ds(c * PATCH, PATCH)], out.at[m, c, 0], sem.at[m, c]
                )
            )
    for copy in copies:
        copy.start()
    for copy in copies:
        copy.wait()


def per_device(az_size, date_size, image_stack, tap_weights, offsets, matchings):
    lines, samples = image_stack.shape[2:]
    assert image_stack.shape[1] == 1 and lines == PATCH
    matches = matchings.shape[0]
    count = min(matches, date_size)
    columns = samples // HALF + 1
    by_date = matchings.T
    hbm = pl.BlockSpec(memory_space=pltpu.HBM)
    vmem = pl.BlockSpec(memory_space=pltpu.VMEM)
    smem = pl.BlockSpec(memory_space=pltpu.SMEM)
    constants = tables()
    extra = [by_date] if count < date_size else []
    results = pl.pallas_call(
        functools.partial(stack_kernel, az_size, date_size, count),
        out_shape=pltpu.VMEM((count, 2 * lines, samples), jnp.float32),
        in_specs=[hbm] * 4 + [smem] * len(extra),
        out_specs=vmem,
        scratch_shapes=[
            pltpu.VMEM(image_stack.shape, jnp.float32),
            pltpu.VMEM(tap_weights.shape, jnp.float32),
            pltpu.VMEM(offsets.shape, jnp.int32),
            pltpu.VMEM(constants.shape, jnp.bfloat16),
            pltpu.VMEM((2, 2, lines, samples), jnp.bfloat16),
            pltpu.VMEM((2, HALF, 4 * HALF), jnp.bfloat16),
            pltpu.VMEM((TAPS, 2 * lines), jnp.float32),
            pltpu.VMEM((2, 2, lines + 2 * REACH, samples), jnp.bfloat16),
            pltpu.VMEM((3, 2, HALF, 4 * HALF), jnp.bfloat16),
            pltpu.VMEM((3, TAPS, 2 * lines), jnp.float32),
            pltpu.VMEM((date_size, samples + 2 * HALF, 8 * HALF), jnp.bfloat16),
            pltpu.VMEM((columns, 2 * PATCH, LANES), jnp.float32),
            pltpu.VMEM((columns * PATCH, LANES), jnp.bfloat16),
            pltpu.VMEM((columns, 2 * PATCH, LANES), jnp.bfloat16),
            pltpu.VMEM((samples, 2 * LANES), jnp.bfloat16),
            pltpu.SemaphoreType.DMA((4,)),
            pltpu.SemaphoreType.DMA((date_size, 3, 3)),
            pltpu.SemaphoreType.DMA((date_size, 3, 3)),
        ],
        compiler_params=pltpu.CompilerParams(collective_id=0, has_side_effects=True),
    )(image_stack, tap_weights, offsets, jnp.asarray(constants), *extra)
    return pl.pallas_call(
        functools.partial(spread_kernel, date_size, count),
        out_shape=jax.ShapeDtypeStruct((matches, 2, 1, lines, samples), jnp.float32),
        in_specs=[smem, vmem],
        out_specs=hbm,
        scratch_shapes=[pltpu.SemaphoreType.DMA((matches, 2))],
        compiler_params=pltpu.CompilerParams(vmem_limit_bytes=16 << 20),
    )(by_date, results)


def solution(mesh):
    placed = (
        P(None, ("parts", "date"), "az", "rg"),
        P(None, ("parts", "date"), "az"),
        P(("parts", "date"), "az"),
        P(),
    )
    assert mesh.shape["rg"] == 2
    return jax.shard_map(
        functools.partial(per_device, mesh.shape["az"], mesh.shape["date"]),
        mesh=mesh,
        in_specs=placed,
        out_specs=P(None, None, ("parts", "date"), "az", "rg"),
        check_vma=False,
    )
```

```python
import functools
import math

import jax
import jax.numpy as jnp
import ml_dtypes
import numpy as np
from jax import lax
from jax.experimental import pallas as pl
from jax.experimental.pallas import tpu as pltpu
from jax.sharding import PartitionSpec as P

TAPS = 8
SHIFT_MAX = 12
PATCH = 64
HALF = PATCH // 2
RIM = SHIFT_MAX + TAPS // 2
GROUPS = 4
LANES = GROUPS * PATCH
MESH = pl.DeviceIdType.MESH
BF16 = ml_dtypes.bfloat16
PLACE = {1: 0, 0: 1, -1: 2}


def fourier_table(sine_sign, table_scale):
    ids = np.arange(PATCH)
    angles = ((ids[:, None] * ids[None, :]) % PATCH) * (2.0 * math.pi / PATCH)
    cosine = np.cos(angles) * table_scale
    sine = np.sin(angles) * (sine_sign * table_scale)
    table = np.block([[cosine, -sine], [sine, cosine]]).astype(np.float32)
    return table.astype(BF16).astype(np.float32)


def tables():
    forward = fourier_table(1.0, 1.0)
    inverse = fourier_table(-1.0, 1.0 / PATCH)
    window = np.sin(math.pi * (np.arange(PATCH, dtype=np.float32) + 0.5) / PATCH) ** 2
    wide = 2 * PATCH
    line_in = np.zeros((2, wide, 2, GROUPS, PATCH), np.float32)
    line_out = np.zeros((2, PATCH, 2, GROUPS, PATCH), np.float32)
    split_f = forward.reshape(2, PATCH, 2, PATCH)
    split_i = inverse.reshape(2, PATCH, 2, PATCH)
    for r in range(3):
        line_in[:, r * HALF : r * HALF + PATCH, :, r] = split_f
        for line in range(PATCH):
            u = line + HALF - HALF * r
            if 0 <= u < PATCH:
                line_out[:, line, :, r] = split_i[:, :, :, u].transpose(2, 0, 1) * window[u]
    line_in = line_in.reshape(2 * wide, 2 * LANES).astype(BF16)
    line_out = line_out.reshape(wide, 2 * LANES)
    high = line_out.astype(BF16)
    low = (line_out - high.astype(np.float32)).astype(BF16)
    ids = np.arange(LANES)
    gap = (ids[:, None] - ids[None, :]) % PATCH
    same = ids[:, None] // PATCH == ids[None, :] // PATCH
    ring = (((gap <= 1) | (gap == PATCH - 1)) & same).astype(BF16)
    turns = np.concatenate([forward.T, inverse.T], axis=0).astype(BF16)
    rows = np.broadcast_to(np.tile(window, 2)[:, None], (wide, wide)).astype(np.float32)
    rows_high = rows.astype(BF16)
    rows_low = (rows - rows_high.astype(np.float32)).astype(BF16)
    last = np.concatenate([ring, turns, np.concatenate([rows_high, rows_low], axis=0)], axis=1)
    return np.concatenate([line_in, high, low, last], axis=0)


def stack_kernel(
    az_size, date_size, count, image_hbm, taps_hbm, offsets_hbm, table_hbm, *rest,
):
    if count < date_size:
        matchings, *rest = rest
    (
        out, image, taps, offsets, table, halo, tile, pack, wide, marg, spec, power_sum, shaped,
        back, load_sem, halo_send, halo_recv, send_sem, recv_sem,
    ) = rest
    a = lax.axis_index("az")
    d = lax.axis_index("date")
    g = lax.axis_index("rg")
    lines = image.shape[2]
    samples = image.shape[3]
    loads = [
        pltpu.make_async_copy(source, target, load_sem.at[i])
        for i, (source, target) in enumerate(
            ((offsets_hbm, offsets), (taps_hbm, taps), (image_hbm, image), (table_hbm, table))
        )
    ]
    has_up = a > 0
    has_down = a < az_size - 1
    exists = {-1: has_up, 0: None, 1: has_down}

    def guarded(step, body):
        if exists[step] is None:
            body()
        else:
            pl.when(exists[step])(body)

    def place_at(az_step, date_step, other):
        return {
            "az": a + az_step,
            "date": lax.rem(d + date_step, date_size),
            "rg": 1 - g if other else g,
        }

    peers = [
        (o, t, k) for o in (-1, 0, 1) for t in range(date_size) for k in (0, 1)
        if (o, t, k) != (0, 0, 0)
    ]
    barrier = pltpu.get_barrier_semaphore()
    for o, t, k in peers:
        guarded(o, lambda o=o, t=t, k=k: pl.semaphore_signal(
            barrier, inc=1, device_id=place_at(o, t, k), device_id_type=MESH))
    for load in loads:
        load.start()
    rows_near = 1 + has_up.astype(jnp.int32) + has_down.astype(jnp.int32)
    pl.semaphore_wait(barrier, rows_near * (2 * date_size) - 1)

    def halo_copy(step, target_step):
        first = lines - RIM if step == 1 else 0
        slot = 0 if step == 1 else 1
        return pltpu.make_async_remote_copy(
            src_ref=image_hbm.at[:, 0, pl.ds(first, RIM), :],
            dst_ref=halo.at[slot],
            send_sem=halo_send.at[slot],
            recv_sem=halo_recv.at[slot],
            device_id=place_at(target_step, 0, 0),
            device_id_type=MESH,
        )

    for step in (1, -1):
        guarded(step, lambda step=step: halo_copy(step, step).start())

    @pl.when(jnp.logical_not(has_up))
    def _():
        halo[0] = jnp.zeros(halo.shape[1:], halo.dtype)
        wide[:, :, 0:HALF] = jnp.zeros((date_size, 2, HALF, wide.shape[3]), wide.dtype)
        marg[:, 0] = jnp.zeros((date_size,) + marg.shape[2:], marg.dtype)

    @pl.when(jnp.logical_not(has_down))
    def _():
        halo[1] = jnp.zeros(halo.shape[1:], halo.dtype)
        wide[:, :, 3 * HALF :] = jnp.zeros((date_size, 2, HALF, wide.shape[3]), wide.dtype)
        marg[:, 2] = jnp.zeros((date_size,) + marg.shape[2:], marg.dtype)

    for load in loads[:3]:
        load.wait()
    span = lines + 2 * RIM
    source = lax.broadcasted_iota(jnp.int32, (span, lines), 0)
    place = lax.broadcasted_iota(jnp.int32, (span, lines), 1)
    gap = source - place - (RIM - (TAPS // 2 - 1)) - offsets[0:1, :]
    band = jnp.zeros((span, lines), jnp.float32)
    for k in range(TAPS):
        band = jnp.where(gap == k, taps[k], band)

    def split(value):
        high = value.astype(jnp.bfloat16)
        return high, (value - high.astype(jnp.float32)).astype(jnp.bfloat16)

    bands = jnp.concatenate(split(band), axis=1)

    guarded(-1, lambda: halo_copy(1, -1).wait_recv())
    guarded(1, lambda: halo_copy(-1, 1).wait_recv())
    stacked = jnp.concatenate(
        [
            jnp.concatenate([halo[0, c], image[c, 0], halo[1, c]], axis=0)
            for c in range(2)
        ],
        axis=1,
    )
    both = None
    for piece in split(stacked):
        product = lax.dot_general(
            bands, piece, (((0,), (0,)), ((), ())), preferred_element_type=jnp.float32
        )
        product = product[:lines] + product[lines:]
        both = product if both is None else both + product
    results = [both[:, :samples], both[:, samples:]]
    parts = []
    for c in range(2):
        wide[0, c, HALF : HALF + lines] = results[c].astype(jnp.bfloat16)
        tile[c] = results[c].astype(jnp.bfloat16)
        edge = jnp.where(g == 0, results[c][:, samples - HALF :], results[c][:, :HALF])
        parts += [edge[:HALF], edge[HALF:]]
    pack[...] = jnp.concatenate(parts, axis=1).astype(jnp.bfloat16)

    taken = {1: (HALF, HALF, 0), 0: (0, lines, HALF), -1: (0, HALF, HALF + lines)}

    def tile_copy(o, t, other, target):
        slot = (date_size - t) % date_size
        spot = PLACE[o]
        if other:
            src, dst = pack, marg.at[slot, spot]
        else:
            first, size, land = taken[o]
            src = tile.at[:, pl.ds(first, size), :]
            dst = wide.at[slot, :, pl.ds(land, size), :]
        return pltpu.make_async_remote_copy(
            src_ref=src, dst_ref=dst,
            send_sem=send_sem.at[t, spot, other],
            recv_sem=recv_sem.at[slot, spot, other],
            device_id=target, device_id_type=MESH,
        )

    order = sorted(peers, key=lambda p: (p[1], abs(p[0]), p[2]))
    for o, t, k in order:
        guarded(o, lambda o=o, t=t, k=k: tile_copy(o, t, k, place_at(o, t, k)).start())

    def arrived(slot):
        for o, t, k in order:
            if (date_size - t) % date_size == slot:
                guarded(-o, lambda o=o, t=t, k=k: tile_copy(
                    o, t, k, place_at(-o, slot, k)).wait_recv())

    def turned(slot):
        core = jnp.concatenate([wide[slot, 0], wide[slot, 1]], axis=0).astype(jnp.float32).T
        blocks = []
        for c in range(2):
            for spot, h in ((0, 1), (1, 0), (1, 1), (2, 0)):
                first = (2 * c + h) * HALF
                blocks.append(marg[slot, spot][:, first : first + HALF].astype(jnp.float32))
        side = jnp.concatenate(blocks, axis=0)
        side = jnp.concatenate([side, jnp.zeros((side.shape[0], 128 - HALF), jnp.float32)], axis=1)
        side = side.T[:HALF]
        zero = jnp.zeros_like(side)
        left = jnp.where(g == 0, zero, side)
        right = jnp.where(g == 0, side, zero)
        return jnp.concatenate([left, core, right], axis=0)

    def filtered(own, other):
        wide_lines = 2 * PATCH
        own_real, own_imag = own[:, :wide_lines], own[:, wide_lines:]
        other_real, other_imag = other[:, :wide_lines], other[:, wide_lines:]
        real_part = own_real * other_real + own_imag * other_imag
        imag_part = own_imag * other_real - own_real * other_imag
        ifg = jnp.concatenate([real_part, imag_part], axis=1).astype(jnp.bfloat16)
        spectra = jnp.dot(
            ifg, table[0 : 2 * wide_lines], preferred_element_type=jnp.float32
        ).astype(jnp.bfloat16)
        ring = table[4 * wide_lines :, 0:LANES]
        forward = table[4 * wide_lines : 5 * wide_lines, LANES : LANES + wide_lines]
        inverse = table[5 * wide_lines :, LANES : LANES + wide_lines]
        rows = [
            table[i * wide_lines : (i + 1) * wide_lines, LANES + wide_lines :].astype(jnp.float32)
            for i in (4, 5)
        ]
        weights = rows[0] + rows[1]
        weights = jnp.concatenate([weights] * (LANES // wide_lines), axis=1)
        columns = samples // HALF + 1
        for q in range(columns):
            rows = spectra[q * HALF : q * HALF + PATCH]
            block = jnp.concatenate([rows[:, :LANES], rows[:, LANES:]], axis=0)
            spectrum = jnp.dot(forward, block, preferred_element_type=jnp.float32)
            spec[q] = spectrum
            real, imag = spectrum[:PATCH], spectrum[PATCH:]
            power = real * real + imag * imag
            summed = power + pltpu.roll(power, 1, 0) + pltpu.roll(power, PATCH - 1, 0)
            power_sum[q * PATCH : (q + 1) * PATCH] = summed.astype(jnp.bfloat16)
        smooth = jnp.dot(power_sum[...], ring, preferred_element_type=jnp.float32)
        gains = lax.rsqrt(lax.rsqrt(1.0 + smooth * (1.0 / (9.0 * PATCH * PATCH))))
        for q in range(columns):
            gain = gains[q * PATCH : (q + 1) * PATCH]
            shaped[q, :PATCH] = (spec[q, :PATCH] * gain).astype(jnp.bfloat16)
            shaped[q, PATCH:] = (spec[q, PATCH:] * gain).astype(jnp.bfloat16)
        held = None
        for q in range(columns):
            ranged = jnp.dot(inverse, shaped[q], preferred_element_type=jnp.float32) * weights
            if held is not None:
                for c in range(2):
                    joined = held[c] + ranged[c * PATCH : c * PATCH + HALF]
                    back[(q - 1) * HALF : q * HALF, c * LANES : (c + 1) * LANES] = joined.astype(
                        jnp.bfloat16
                    )
            held = [ranged[c * PATCH + HALF : (c + 1) * PATCH] for c in range(2)]
        split = lax.dot_general(
            table[2 * wide_lines : 4 * wide_lines], back[...], (((1,), (1,)), ((), ())),
            preferred_element_type=jnp.float32,
        )
        return split[:wide_lines] + split[wide_lines:]

    loads[3].wait()
    arrived(0)
    own = turned(0)
    if count == date_size:
        for j in range(count):
            if j:
                arrived(j)
            out[j] = filtered(own, turned(j) if j else own)
    else:
        for j in range(1, date_size):
            arrived(j)
        for m in range(count):
            slot = lax.rem(matchings[d, m] - d + date_size, date_size)
            out[m] = filtered(own, turned(slot))

    for step in (1, -1):
        guarded(step, lambda step=step: halo_copy(step, step).wait_send())
    for o, t, k in order:
        guarded(o, lambda o=o, t=t, k=k: tile_copy(o, t, k, place_at(o, t, k)).wait_send())


def spread_kernel(date_size, count, matchings, results, out, sem):
    d = lax.axis_index("date")
    copies = []
    for m in range(out.shape[0]):
        spot = m
        if count == date_size:
            spot = lax.rem(matchings[d, m] - d + date_size, date_size)
        for c in range(2):
            copies.append(
                pltpu.make_async_copy(
                    results.at[spot, pl.ds(c * PATCH, PATCH)], out.at[m, c, 0], sem.at[m, c]
                )
            )
    for copy in copies:
        copy.start()
    for copy in copies:
        copy.wait()


def per_device(az_size, date_size, image_stack, tap_weights, offsets, matchings):
    lines, samples = image_stack.shape[2:]
    assert image_stack.shape[1] == 1 and lines == PATCH
    matches = matchings.shape[0]
    count = min(matches, date_size)
    columns = samples // HALF + 1
    by_date = matchings.T
    hbm = pl.BlockSpec(memory_space=pltpu.HBM)
    vmem = pl.BlockSpec(memory_space=pltpu.VMEM)
    smem = pl.BlockSpec(memory_space=pltpu.SMEM)
    constants = tables()
    extra = [by_date] if count < date_size else []
    results = pl.pallas_call(
        functools.partial(stack_kernel, az_size, date_size, count),
        out_shape=pltpu.VMEM((count, 2 * lines, samples), jnp.float32),
        in_specs=[hbm] * 4 + [smem] * len(extra),
        out_specs=vmem,
        scratch_shapes=[
            pltpu.VMEM(image_stack.shape, jnp.float32),
            pltpu.VMEM(tap_weights.shape, jnp.float32),
            pltpu.VMEM(offsets.shape, jnp.int32),
            pltpu.VMEM(constants.shape, jnp.bfloat16),
            pltpu.VMEM((2, 2, RIM, samples), jnp.float32),
            pltpu.VMEM((2, lines, samples), jnp.bfloat16),
            pltpu.VMEM((HALF, 4 * HALF), jnp.bfloat16),
            pltpu.VMEM((date_size, 2, 4 * HALF, samples), jnp.bfloat16),
            pltpu.VMEM((date_size, 3, HALF, 4 * HALF), jnp.bfloat16),
            pltpu.VMEM((columns, 2 * PATCH, LANES), jnp.float32),
            pltpu.VMEM((columns * PATCH, LANES), jnp.bfloat16),
            pltpu.VMEM((columns, 2 * PATCH, LANES), jnp.bfloat16),
            pltpu.VMEM((samples, 2 * LANES), jnp.bfloat16),
            pltpu.SemaphoreType.DMA((4,)),
            pltpu.SemaphoreType.DMA((2,)),
            pltpu.SemaphoreType.DMA((2,)),
            pltpu.SemaphoreType.DMA((date_size, 3, 2)),
            pltpu.SemaphoreType.DMA((date_size, 3, 2)),
        ],
        compiler_params=pltpu.CompilerParams(collective_id=0, has_side_effects=True),
    )(image_stack, tap_weights, offsets, jnp.asarray(constants), *extra)
    return pl.pallas_call(
        functools.partial(spread_kernel, date_size, count),
        out_shape=jax.ShapeDtypeStruct((matches, 2, 1, lines, samples), jnp.float32),
        in_specs=[smem, vmem],
        out_specs=hbm,
        scratch_shapes=[pltpu.SemaphoreType.DMA((matches, 2))],
        compiler_params=pltpu.CompilerParams(vmem_limit_bytes=16 << 20),
    )(by_date, results)


def solution(mesh):
    placed = (
        P(None, ("parts", "date"), "az", "rg"),
        P(None, ("parts", "date"), "az"),
        P(("parts", "date"), "az"),
        P(),
    )
    assert mesh.shape["rg"] == 2
    return jax.shard_map(
        functools.partial(per_device, mesh.shape["az"], mesh.shape["date"]),
        mesh=mesh,
        in_specs=placed,
        out_specs=P(None, None, ("parts", "date"), "az", "rg"),
        check_vma=False,
    )
```
